128 devices in a mesh: rows: 32 (over z, x, core), sk: 4 (over y).
Axes of the slice: x: 4, y: 4, z: 4, core: 2. Of those that a mesh axis runs over, the one named last changes fastest.
Arguments:
- panel: float32 [64, 1048576], P(None, ('rows', 'sk')), may hold values from -200 to 200
- signs: int32 [1048576], P(('rows', 'sk')), may hold values from -1 to 1
- sample_device: int32 [16384, 1], replicated, may hold values from 0 to 127; in each aligned block of 128 rows (0 to 127, 128 to 255, ...) at most 4 rows name the same one
- sample_offset: int32 [16384], replicated, may hold values from 0 to 8191
Outputs:
- mixed: float32 [64, 1048576], P(None, ('rows', 'sk'))
- r_factor: float32 [64, 64], replicated
- whitened: float32 [64, 16384], P(None, ('rows', 'sk'))
The draws below stay inside these ranges and needn't reach their ends.
Inputs may be any that keep to these rules, and one draw needn't show every extreme that they name: `sample_device`: among the sample positions j * 128 to (j + 1) * 128 - 1 of any j, no device number appears more than 4 times, and some block reaches it.
All inputs are finite; a program needn't handle non-finite values.
Results may differ from the reference program's by a relative error of at most 0.0003.
Values sent between devices are 32-bit elements; how exact they have to be, the bound alone decides.
A program may use at most 64 MiB of HBM per device.

```python
import math
import jax
import jax.numpy as jnp
import numpy as np
from jax import lax

COLS = 64
ROWS_DEV = 8192
S_DEV = 128
CAP = 4
TOTAL_ROWS = 1048576
SAMPLES = 16384
N_ROWS = 32
N_SK = 4


def draw_panel(key, part):
    first_key, second_key, third_key = jax.random.split(key, 3)
    base = jnp.clip(jax.random.normal(first_key, (COLS, TOTAL_ROWS), jnp.float32), -6.0, 6.0)
    shared = 0.6
    row_scale = jnp.exp(jax.random.uniform(second_key, (1, TOTAL_ROWS), jnp.float32) * math.log(10.0))
    col_scale = jnp.exp(jax.random.uniform(third_key, (COLS, 1), jnp.float32) * math.log(10.0))
    return (base + shared * base[:1, :]) * row_scale * col_scale * 0.125


def draw_signs(key, part):
    return (2 * jax.random.randint(key, (TOTAL_ROWS,), 0, 2) - 1).astype(jnp.int32)


def with_ends(array, rng, smallest, largest):
    longest = array.shape.index(max(array.shape))
    spots = []
    for shift in (0, 1):
        where = [jax.random.randint(jax.random.fold_in(rng, axis), (), 0, length) for axis, length in enumerate(array.shape)]
        where[longest] = (where[longest] + shift) % array.shape[longest]
        spots.append(tuple(where))
    return array.at[spots[0]].set(smallest).at[spots[1]].set(largest)


def shared_out(stream_key, own, number, rows, amount, top, limit, lean):
    sequence = jax.random.permutation(stream_key, amount)
    heavy_load, usual = load_shares(amount, rows * top, limit, lean, True), load_shares(amount, rows * top, limit, lean, False)
    places = jnp.arange(amount)

    def named(lengths, rotation):
        used = int((lengths > 0).sum())
        fixed = max(1, used // 4)
        shifted = fixed + (places - fixed + rotation * (used - fixed)) % max(1, amount - fixed)
        return jnp.zeros((amount,), jnp.int32).at[sequence[jnp.where(places < fixed, places, shifted)]].set(jnp.asarray(lengths, jnp.int32))

    lengths = jnp.where(number % 4 == 0, named(heavy_load, number // 4), named(usual, number - number // 4 - 1))
    mixed = jax.random.permutation(jax.random.fold_in(own, 3), amount)
    giver, sink = mixed[0:amount // 2 * 2:2], mixed[1:amount // 2 * 2:2]
    slack = jnp.minimum(lengths[giver] - 1, limit - lengths[sink]) // 2
    slack = jnp.where((giver == sequence[0]) | (sink == sequence[0]) | (lengths[sink] == 0), 0, jnp.maximum(slack, 0))
    shifted = jax.random.randint(jax.random.fold_in(own, 4), (amount // 2,), 0, 1 << 20) % (slack + 1)
    lengths = lengths.at[giver].add(-shifted).at[sink].add(shifted)
    labels = jnp.searchsorted(jnp.cumsum(lengths), jnp.arange(rows * top), side="right").astype(jnp.int32)
    grid = labels.reshape(top, rows).T
    grid = grid[jax.random.permutation(jax.random.fold_in(own, 1), rows)]
    rotation = jax.random.randint(jax.random.fold_in(own, 2), (rows, 1), 0, top)
    return jnp.take_along_axis(grid, (jnp.arange(top)[None, :] + rotation) % top, axis=1)


def load_shares(amount, total, reach, slope, full):
    loads = [(1 << 20) // math.isqrt(grade ** slope) + 1 for grade in range(1, amount + 1)]
    largest = reach if full else min(reach, max(-(-total // amount), total * loads[0] // sum(loads)))
    least = 1 if total - largest >= amount - 1 else 0
    counts, surplus = [largest] + [least] * (amount - 1), total - largest - least * (amount - 1)
    while surplus > 0:
        candidates = [i for i in range(1, amount) if counts[i] < largest] or [i for i in range(1, amount) if counts[i] < reach]
        whole, remaining = sum([loads[i] for i in candidates]), surplus
        for i in candidates:
            addition = min(reach - counts[i], max(1, remaining * loads[i] // whole), surplus)
            counts[i] = counts[i] + addition
            surplus = surplus - addition
    return np.array(counts)


def setup_inputs(seed: int = 0) -> dict:
    arg_keys = jax.random.split(jax.random.key(seed), 5)
    panel = draw_panel(jax.random.fold_in(arg_keys[4], 71), 0)
    signs = draw_signs(jax.random.fold_in(arg_keys[4], 71), 0)
    sample_device_keys = jax.random.split(jax.random.fold_in(arg_keys[2], 1), SAMPLES // S_DEV)
    sample_device_turns = jax.random.permutation(jax.random.fold_in(arg_keys[2], 3), SAMPLES // S_DEV)
    sample_device = jax.vmap(lambda own, number: shared_out(jax.random.fold_in(arg_keys[2], 2), own, number, S_DEV, N_ROWS * N_SK, 1, CAP, 2))(sample_device_keys, sample_device_turns).reshape((SAMPLES, 1))
    sample_offset = with_ends(jax.random.randint(arg_keys[3], (SAMPLES,), 0, ROWS_DEV), jax.random.fold_in(arg_keys[3], 1), 0, ROWS_DEV - 1).astype(jnp.int32)
    return dict(panel=panel, signs=signs, sample_device=sample_device, sample_offset=sample_offset)


def hadamard_table(order_size):
    left_ids = jnp.arange(order_size, dtype=jnp.int32)[:, None]
    right_ids = jnp.arange(order_size, dtype=jnp.int32)[None, :]
    common = jnp.bitwise_and(left_ids, right_ids)
    parity = jnp.zeros((order_size, order_size), jnp.int32)
    for bit_number in range(max(order_size.bit_length() - 1, 1)):
        parity = parity + jnp.bitwise_and(jnp.right_shift(common, bit_number), 1)
    return jnp.where(parity % 2 == 0, 1.0, -1.0).astype(jnp.float32)

def householder_r(matrix):
    rows_count, cols_count = matrix.shape
    position = jnp.arange(rows_count, dtype=jnp.int32)

    def reflect(j, current):
        column = lax.dynamic_slice_in_dim(current, j, 1, 1)[:, 0]
        column = jnp.where(position >= j, column, jnp.float32(0.0))
        pivot_value = column[j]
        length = jnp.sqrt(jnp.sum(column * column))
        signed = jnp.where(pivot_value >= 0, jnp.float32(1.0), jnp.float32(-1.0))
        vector = column + signed * length * (position == j).astype(jnp.float32)
        denominator = jnp.sum(vector * vector)
        projection = jnp.dot(vector, current, precision=lax.Precision.HIGHEST)
        return current - vector[:, None] * projection[None, :] * (2.0 / denominator)
    reduced = lax.fori_loop(0, cols_count, reflect, matrix)
    upper = jnp.triu(reduced[:cols_count])
    diag_signs = jnp.where(jnp.diagonal(upper) >= 0, jnp.float32(1.0), jnp.float32(-1.0))
    return upper * diag_signs[:, None]

def forward_solve(upper, values):
    lower = upper.T
    order_size = lower.shape[0]

    def step_row(i, solved):
        row_coef = lax.dynamic_slice_in_dim(lower, i, 1, 0)
        partial_sum = jnp.dot(row_coef, solved, precision=lax.Precision.HIGHEST)
        target = lax.dynamic_slice_in_dim(values, i, 1, 0)
        pivot = lax.dynamic_slice_in_dim(row_coef[0], i, 1, 0)
        new_row = (target - partial_sum) / pivot[0]
        return lax.dynamic_update_slice_in_dim(solved, new_row, i, 0)
    return lax.fori_loop(0, order_size, step_row, jnp.zeros(values.shape, jnp.float32))

def reference(panel, signs, sample_device, sample_offset):
    blocks = N_ROWS * N_SK
    inner = ROWS_DEV // 128
    flipped = panel * signs.astype(jnp.float32)[None, :]
    cube = flipped.reshape(COLS, blocks, inner, 128)
    high = lax.Precision.HIGHEST
    cube = jnp.einsum('cpab,qp->cqab', cube, hadamard_table(blocks), precision=high)
    cube = jnp.einsum('cpab,ea->cpeb', cube, hadamard_table(inner), precision=high)
    cube = jnp.einsum('cpab,db->cpad', cube, hadamard_table(128), precision=high)
    mixed = cube.reshape(COLS, TOTAL_ROWS) * (1.0 / math.sqrt(TOTAL_ROWS))
    global_rows = (sample_device[:, 0] * ROWS_DEV + sample_offset).astype(jnp.int32)
    picked = jnp.take(mixed, global_rows, axis=1)
    sketch = picked * (1.0 / math.sqrt(SAMPLES))
    r_factor = householder_r(sketch.T)
    whitened = forward_solve(r_factor, picked)
    return (mixed, r_factor, whitened)
```

```python
import math

import jax
import jax.numpy as jnp
from jax import lax
from jax.experimental import pallas as pl
from jax.experimental.pallas import tpu as pltpu
from jax.sharding import PartitionSpec as P

F32, BF16, I32 = jnp.float32, jnp.bfloat16, jnp.int32
AXES = ("rows", "sk")
DEVS, COLS, HALF, LANES, CAP = 128, 64, 32, 128, 4


def split3(x):
    top = x.astype(BF16)
    rest = x - top.astype(F32)
    mid = rest.astype(BF16)
    low = (rest - mid.astype(F32)).astype(BF16)
    return top, mid, low


def dot_nn(a, b):
    return lax.dot_general(a, b, (((1,), (0,)), ((), ())), preferred_element_type=F32)


def dot_nt(a, b):
    return lax.dot_general(a, b, (((1,), (1,)), ((), ())), preferred_element_type=F32)


def dot_tn(a, b):
    return lax.dot_general(a, b, (((0,), (0,)), ((), ())), preferred_element_type=F32)


def iota(shape, dim):
    return lax.broadcasted_iota(I32, shape, dim)


def butterflies(values):
    size, step = len(values), 1
    while step < size:
        nxt = list(values)
        for i in range(size):
            if not i & step:
                nxt[i] = values[i] + values[i + step]
                nxt[i + step] = values[i] - values[i + step]
        values, step = nxt, step * 2
    return values


def lane_table():
    k, n = iota((256, 256), 0), iota((256, 256), 1)
    bits = jnp.bitwise_and(k % 128, (n // 128) * 64 + n % 64)
    for shift in (4, 2, 1):
        bits = jnp.bitwise_xor(bits, lax.shift_right_logical(bits, shift))
    sign = 1.0 - 2.0 * jnp.bitwise_and(bits, 1).astype(F32)
    return jnp.where(k // 128 == (n % 128) // 64, sign, 0.0).astype(BF16)


def local_mix(panel, signs, table, send):
    table[...] = lane_table()

    def first(high, carry):
        at = pl.ds(pl.multiple_of(high * 1024, 1024), 1024)
        x = panel[:, at] * signs[:, at].astype(F32)
        lhs = jnp.concatenate(
            [
                jnp.concatenate([x[:HALF, 128 * b : 128 * b + 128], x[HALF:, 128 * b : 128 * b + 128]], axis=1)
                for b in range(8)
            ],
            axis=0,
        )
        weights = table[...]
        top, mid, low = split3(lhs)
        out = dot_nn(low, weights) + dot_nn(mid, weights) + dot_nn(top, weights)
        done = butterflies([out[32 * b : 32 * b + 32] for b in range(8)])
        for b in range(8):
            send[16 * high + 2 * b] = done[b][:, :128]
            send[16 * high + 2 * b + 1] = done[b][:, 128:]
        return carry

    lax.fori_loop(0, 8, first, 0)

    def second(low, carry):
        done = butterflies([send[16 * high + low] for high in range(8)])
        for high in range(8):
            send[16 * high + low] = done[high]
        return carry

    lax.fori_loop(0, 16, second, 0)


def combine(data):
    def first(i, carry):
        high, group = i // 4, i % 4
        at = pl.ds(pl.multiple_of(group * 8, 8), 8)
        done = butterflies([data[16 * high + low, at] for low in range(16)])
        for low in range(16):
            data[16 * high + low, at] = done[low]
        return carry

    lax.fori_loop(0, 32, first, 0)

    def second(low, carry):
        done = butterflies([data[16 * high + low] for high in range(8)])
        for high in range(8):
            data[16 * high + low] = done[high]
        return carry

    lax.fori_loop(0, 16, second, 0)


def unpack(a, b):
    left = iota((HALF, LANES), 1) < 64
    upper = jnp.where(left, a, pltpu.roll(b, 64, 1))
    lower = jnp.where(left, pltpu.roll(a, 64, 1), b)
    return jnp.concatenate([upper, lower], axis=0)


def count_rows(sources, offsets, counts, me):
    counts[...] = jnp.zeros_like(counts)

    def step(i, carry):
        at = pl.ds(pl.multiple_of(i * 8, 8), 8)
        src8, rel8 = sources[at, :], offsets[at, :] - me * 64
        inside = jnp.logical_and(rel8 >= 0, rel8 < 64)
        lane8 = jnp.where(inside, rel8 + jnp.where(src8 >= 64, 64, 0), -1)
        q8 = jnp.bitwise_and(src8, 63)
        total = counts[...]
        for pair in range(4):
            q = jnp.concatenate([q8[2 * pair : 2 * pair + 1], q8[2 * pair + 1 : 2 * pair + 2]], axis=1)
            lane = jnp.concatenate([lane8[2 * pair : 2 * pair + 1], lane8[2 * pair + 1 : 2 * pair + 2]], axis=1)
            left = jnp.where(iota((64, 256), 0) == q, 1.0, 0.0).astype(BF16)
            right = jnp.where(iota((128, 256), 0) == lane, 1.0, 0.0).astype(BF16)
            total = total + dot_nt(left, right)
        counts[...] = total
        return carry

    lax.fori_loop(0, 16, step, 0)


def gram(data, counts, acc):
    acc[...] = jnp.zeros_like(acc)

    def step(i, carry):
        x = jnp.concatenate([unpack(data[2 * i], data[2 * i + 64]), unpack(data[2 * i + 1], data[2 * i + 65])], axis=1)
        w = jnp.concatenate([counts[pl.ds(2 * i, 1), :], counts[pl.ds(2 * i + 1, 1), :]], axis=1)
        plain = jnp.concatenate(split3(x), axis=0)
        weighted = jnp.concatenate(split3(x * w), axis=0)
        acc[...] += dot_nt(weighted, plain)
        return carry

    lax.fori_loop(0, 32, step, 0)
    block = lambda i, j: acc[64 * i : 64 * i + 64, 64 * j : 64 * j + 64]
    small = block(2, 2) + (block(1, 2) + block(2, 1))
    small = small + (block(0, 2) + block(2, 0)) + block(1, 1)
    return small + (block(0, 1) + block(1, 0)) + block(0, 0)


def factor(g):
    sub, lane = iota((COLS, LANES), 0), iota((COLS, LANES), 1)
    m = jnp.concatenate([g, jnp.where(sub == lane, 1.0, 0.0)[:, :64]], axis=1)
    subs = iota((COLS, 1), 0)
    for j in range(COLS):
        pivot_row = m[j : j + 1, :]
        inverse = 1.0 / m[j : j + 1, j : j + 1]
        lead = jnp.where(subs > j, m[:, j : j + 1] * inverse, 0.0)
        m = m - lead * pivot_row
    diagonal = jnp.sum(jnp.where(sub == lane, m, 0.0), axis=1, keepdims=True)
    scaled = m / jnp.sqrt(diagonal)
    return jnp.where(jnp.logical_or(lane >= sub, lane >= 64), scaled, 0.0)


def earlier():
    return jnp.where(iota((128, 128), 0) < iota((128, 128), 1), 1.0, 0.0).astype(BF16)


def slot_places(sources, offsets, me):
    mine = sources[...] == me
    rank = dot_nn(jnp.where(mine, 1.0, 0.0).astype(BF16), earlier())
    high = (offsets[...] // 128).astype(F32)
    low = (offsets[...] % 128).astype(F32)
    ones = jnp.ones((8, 128), BF16)
    places = []
    for r in range(CAP):
        chosen = jnp.logical_and(mine, rank == float(r))
        places.append(
            tuple(dot_nt(ones, jnp.where(chosen, v, 0.0).astype(BF16)).astype(I32) for v in (high, low))
        )
    return places


def finish(back, places, mixed, scale):
    highs = [jnp.concatenate([high] * 8, axis=0) for high, _ in places]
    lows = [jnp.concatenate([low] * 8, axis=0) for _, low in places]

    def step(b, picked):
        x = unpack(back[2 * b], back[2 * b + 1]) * scale
        mixed[:, pl.ds(pl.multiple_of(b * 128, 128), 128)] = x
        return tuple(
            jnp.where(high == b, jnp.take_along_axis(x, low, axis=1, mode="promise_in_bounds"), old)
            for high, low, old in zip(highs, lows, picked)
        )

    return lax.fori_loop(0, 64, step, tuple(jnp.zeros((COLS, LANES), F32) for _ in range(CAP)))


def exact6(a, b, dot):
    a1, a2, a3 = split3(a)
    b1, b2, b3 = split3(b)
    small = dot(a2, b2) + (dot(a1, b3) + dot(a3, b1))
    return small + (dot(a1, b2) + dot(a2, b1)) + dot(a1, b1)


def whiten_slots(picked, inverse, out):
    done = [exact6(p.T, inverse, dot_nt) for p in picked]
    for pair in range(2):
        out[:, pair, :] = jnp.concatenate(done[2 * pair : 2 * pair + 2], axis=1)


def place_samples(incoming, own):
    hot = iota((128, 128), 0) == own
    flag = jnp.where(hot, 1.0, 0.0)
    rank = dot_nn(flag.astype(BF16), earlier())
    total = jnp.zeros((COLS, LANES), F32)
    for pair in range(2):
        top, mid, low = split3(incoming[:, pair, :])
        for half in range(2):
            chosen = jnp.where(rank == float(2 * pair + half), flag, 0.0).astype(BF16)
            got = dot_tn(low, chosen) + dot_tn(mid, chosen) + dot_tn(top, chosen)
            total = total + got[64 * half : 64 * half + 64]
    return total


def my_id():
    return lax.axis_index("rows") * 4 + lax.axis_index("sk")


def call(body, out, *args, scratch=(), smem=()):
    spec = pl.BlockSpec(memory_space=pltpu.VMEM)
    return pl.pallas_call(
        body,
        out_shape=out,
        in_specs=[pl.BlockSpec(memory_space=pltpu.SMEM) if i in smem else spec for i in range(len(args))],
        out_specs=jax.tree.map(lambda _: spec, out),
        scratch_shapes=list(scratch),
        compiler_params=pltpu.CompilerParams(vmem_limit_bytes=56 << 20),
    )(*args)


def shape(*dims):
    return jax.ShapeDtypeStruct(dims, F32)


def local(panel, signs, sample_device, sample_offset):
    me = my_id().astype(I32).reshape(1)
    sources = sample_device.reshape(128, 128)
    offsets = sample_offset.reshape(128, 128)

    def mix(panel_ref, signs_ref, send, table):
        local_mix(panel_ref, signs_ref, table, send)

    blocks = shape(DEVS, HALF, LANES)
    send = call(mix, blocks, panel, signs.reshape(1, -1), scratch=[pltpu.VMEM((256, 256), BF16)])
    arrived = lax.all_to_all(send, AXES, split_axis=0, concat_axis=0, tiled=True)

    def middle(me_ref, arrived_ref, src, off, data, g, counts, acc):
        data[...] = arrived_ref[...]
        combine(data)
        count_rows(src, off, counts, me_ref[0])
        g[...] = gram(data, counts, acc)

    data, g = call(
        middle, (blocks, shape(64, 64)), me, arrived, sources, offsets,
        scratch=[pltpu.VMEM((64, 128), F32), pltpu.VMEM((192, 192), F32)], smem=(0,),
    )
    back = lax.all_to_all(data, AXES, split_axis=0, concat_axis=0, tiled=True)
    total = lax.psum(g, AXES)

    def chol(g_ref, out):
        out[...] = factor(g_ref[...] * (2.0**-34))

    both = call(chol, shape(64, 128), total)

    def last(me_ref, back_ref, src, off, both_ref, mixed, slots):
        places = slot_places(src, off, me_ref[0])
        picked = finish(back_ref, places, mixed, 2.0**-10)
        whiten_slots(picked, both_ref[:, 64:], slots)

    mixed, slots = call(
        last, (shape(64, 8192), shape(DEVS, 2, LANES)), me, back, sources, offsets, both, smem=(0,)
    )
    incoming = lax.all_to_all(slots, AXES, split_axis=0, concat_axis=0, tiled=True)
    own = lax.dynamic_slice_in_dim(sources, me[0], 1, 0)

    def place(incoming_ref, own_ref, out):
        out[...] = place_samples(incoming_ref, own_ref[...])

    whitened = call(place, shape(64, 128), incoming, own)
    return mixed, both[:, :64], whitened


def solution(mesh):
    return jax.shard_map(
        local,
        mesh=mesh,
        in_specs=(P(None, AXES), P(AXES), P(), P()),
        out_specs=(P(None, AXES), P(), P(None, AXES)),
        check_vma=False,
    )
```

```python
import jax
import jax.numpy as jnp
from jax import lax
from jax.experimental import pallas as pl
from jax.experimental.pallas import tpu as pltpu
from jax.sharding import PartitionSpec as P

F32, BF16, I32 = jnp.float32, jnp.bfloat16, jnp.int32
AXES = ("rows", "sk")
DEVS, COLS, HALF, LANES, CAP = 128, 64, 32, 128, 4


def split3(x):
    top = x.astype(BF16)
    rest = x - top.astype(F32)
    mid = rest.astype(BF16)
    low = (rest - mid.astype(F32)).astype(BF16)
    return top, mid, low


def dot_nn(a, b):
    return lax.dot_general(a, b, (((1,), (0,)), ((), ())), preferred_element_type=F32)


def dot_nt(a, b):
    return lax.dot_general(a, b, (((1,), (1,)), ((), ())), preferred_element_type=F32)


def dot_tn(a, b):
    return lax.dot_general(a, b, (((0,), (0,)), ((), ())), preferred_element_type=F32)


def iota(shape, dim):
    return lax.broadcasted_iota(I32, shape, dim)


def butterflies(values):
    size, step = len(values), 1
    while step < size:
        nxt = list(values)
        for i in range(size):
            if not i & step:
                nxt[i] = values[i] + values[i + step]
                nxt[i + step] = values[i] - values[i + step]
        values, step = nxt, step * 2
    return values


def lane_table():
    k, n = iota((256, 256), 0), iota((256, 256), 1)
    bits = jnp.bitwise_and(k % 128, (n // 128) * 64 + n % 64)
    for shift in (4, 2, 1):
        bits = jnp.bitwise_xor(bits, lax.shift_right_logical(bits, shift))
    sign = 1.0 - 2.0 * jnp.bitwise_and(bits, 1).astype(F32)
    return jnp.where(k // 128 == (n % 128) // 64, sign, 0.0).astype(BF16)
SPLIT = 72


PARTS = 2
ROWS = HALF // PARTS
MESH = pl.DeviceIdType.MESH


def local_mix(part, panel, signs, table, send):
    at_rows = pl.ds(part * ROWS, ROWS)

    def first(high, carry):
        at = pl.ds(pl.multiple_of(high * 1024, 1024), 1024)
        sign = signs[:, at].astype(F32)
        upper = panel[part * ROWS : part * ROWS + ROWS, at] * sign
        lower = panel[HALF + part * ROWS : HALF + part * ROWS + ROWS, at] * sign
        lhs = jnp.concatenate(
            [
                jnp.concatenate([upper[:, 128 * b : 128 * b + 128], lower[:, 128 * b : 128 * b + 128]], axis=1)
                for b in range(8)
            ],
            axis=0,
        )
        weights = table[...]
        top, mid, low = split3(lhs)
        out = dot_nn(low, weights) + dot_nn(mid, weights) + dot_nn(top, weights)
        done = butterflies([out[ROWS * b : ROWS * b + ROWS] for b in range(8)])
        for b in range(8):
            send[16 * high + 2 * b, at_rows] = done[b][:, :128]
            send[16 * high + 2 * b + 1, at_rows] = done[b][:, 128:]
        return carry

    lax.fori_loop(0, 8, first, 0)

    def second(low, carry):
        done = butterflies([send[16 * high + low, at_rows] for high in range(8)])
        for high in range(8):
            send[16 * high + low, at_rows] = done[high]
        return carry

    lax.fori_loop(0, 16, second, 0)


def combine(part, data):
    def first(i, carry):
        high, group = i // (ROWS // 8), i % (ROWS // 8)
        at = pl.ds(pl.multiple_of(part * ROWS + group * 8, 8), 8)
        done = butterflies([data[16 * high + low, at] for low in range(16)])
        for low in range(16):
            data[16 * high + low, at] = done[low]
        return carry

    lax.fori_loop(0, 8 * (ROWS // 8), first, 0)
    at_rows = pl.ds(part * ROWS, ROWS)

    def second(low, carry):
        done = butterflies([data[16 * high + low, at_rows] for high in range(8)])
        for high in range(8):
            data[16 * high + low, at_rows] = done[high]
        return carry

    lax.fori_loop(0, 16, second, 0)


def unpack(a, b):
    left = iota((HALF, LANES), 1) < 64
    upper = jnp.where(left, a, pltpu.roll(b, 64, 1))
    lower = jnp.where(left, pltpu.roll(a, 64, 1), b)
    return jnp.concatenate([upper, lower], axis=0)


def count_rows(sources, offsets, counts, me):
    counts[...] = jnp.zeros_like(counts)

    def step(i, carry):
        at = pl.ds(pl.multiple_of(i * 8, 8), 8)
        src8, rel8 = sources[at, :], offsets[at, :] - me * 64
        inside = jnp.logical_and(rel8 >= 0, rel8 < 64)
        lane8 = jnp.where(inside, rel8 + jnp.where(src8 >= 64, 64, 0), -1)
        q8 = jnp.bitwise_and(src8, 63)
        total = counts[...]
        for pair in range(4):
            q = jnp.concatenate([q8[2 * pair : 2 * pair + 1], q8[2 * pair + 1 : 2 * pair + 2]], axis=1)
            lane = jnp.concatenate([lane8[2 * pair : 2 * pair + 1], lane8[2 * pair + 1 : 2 * pair + 2]], axis=1)
            left = jnp.where(iota((64, 256), 0) == q, 1.0, 0.0).astype(BF16)
            right = jnp.where(iota((128, 256), 0) == lane, 1.0, 0.0).astype(BF16)
            total = total + dot_nt(left, right)
        counts[...] = total
        return carry

    lax.fori_loop(0, 16, step, 0)


def gram(data, counts, acc):
    acc[...] = jnp.zeros_like(acc)

    def step(i, carry):
        x = jnp.concatenate([unpack(data[2 * i], data[2 * i + 64]), unpack(data[2 * i + 1], data[2 * i + 65])], axis=1)
        w = jnp.concatenate([counts[pl.ds(2 * i, 1), :], counts[pl.ds(2 * i + 1, 1), :]], axis=1)
        plain = jnp.concatenate(split3(x), axis=0)
        weighted = jnp.concatenate(split3(x * w), axis=0)
        acc[...] += dot_nt(weighted, plain)
        return carry

    lax.fori_loop(0, 32, step, 0)
    block = lambda i, j: acc[64 * i : 64 * i + 64, 64 * j : 64 * j + 64]
    small = block(2, 2) + (block(1, 2) + block(2, 1))
    small = small + (block(0, 2) + block(2, 0)) + block(1, 1)
    return small + (block(0, 1) + block(1, 0)) + block(0, 0)


def factor(g):
    sub, lane = iota((COLS, LANES), 0), iota((COLS, LANES), 1)
    m = jnp.concatenate([g, jnp.where(sub == lane, 1.0, 0.0)[:, :64]], axis=1)
    subs = iota((COLS, 1), 0)
    for j in range(COLS):
        pivot_row = m[j : j + 1, :]
        inverse = 1.0 / m[j : j + 1, j : j + 1]
        lead = jnp.where(subs > j, m[:, j : j + 1] * inverse, 0.0)
        m = m - lead * pivot_row
    diagonal = jnp.sum(jnp.where(sub == lane, m, 0.0), axis=1, keepdims=True)
    scaled = m / jnp.sqrt(diagonal)
    return jnp.where(jnp.logical_or(lane >= sub, lane >= 64), scaled, 0.0)


def earlier():
    return jnp.where(iota((128, 128), 0) < iota((128, 128), 1), 1.0, 0.0).astype(BF16)


def slot_places(sources, offsets, me):
    mine = sources[...] == me
    rank = dot_nn(jnp.where(mine, 1.0, 0.0).astype(BF16), earlier())
    high = (offsets[...] // 128).astype(F32)
    low = (offsets[...] % 128).astype(F32)
    ones = jnp.ones((8, 128), BF16)
    places = []
    for r in range(CAP):
        chosen = jnp.logical_and(mine, rank == float(r))
        places.append(
            tuple(dot_nt(ones, jnp.where(chosen, v, 0.0).astype(BF16)).astype(I32) for v in (high, low))
        )
    return places


def unpack_part(part, back, mixed, scale):
    def step(b, carry):
        at = pl.ds(pl.multiple_of(b * 128, 128), 128)
        one, two = back[2 * b, pl.ds(part * ROWS, ROWS)], back[2 * b + 1, pl.ds(part * ROWS, ROWS)]
        left = iota((ROWS, LANES), 1) < 64
        mixed[part * ROWS : part * ROWS + ROWS, at] = jnp.where(left, one, pltpu.roll(two, 64, 1)) * scale
        mixed[HALF + part * ROWS : HALF + part * ROWS + ROWS, at] = jnp.where(left, pltpu.roll(one, 64, 1), two) * scale
        return carry

    lax.fori_loop(0, 64, step, 0)


def pick_part(part, mixed, places, picked):
    for r, (high, low) in enumerate(places):
        high = jnp.concatenate([high] * (ROWS // 8), axis=0)
        low = jnp.concatenate([low] * (ROWS // 8), axis=0)

        def step(i, found):
            for k in range(4):
                b = 4 * i + k
                at = pl.ds(pl.multiple_of(b * 128, 128), 128)
                found = tuple(
                    jnp.where(
                        high == b,
                        jnp.take_along_axis(mixed[base : base + ROWS, at], low, axis=1, mode="promise_in_bounds"),
                        old,
                    )
                    for base, old in zip((part * ROWS, HALF + part * ROWS), found)
                )
            return found

        zero = jnp.zeros((ROWS, LANES), F32)
        upper, lower = lax.fori_loop(0, 16, step, (zero, zero))
        picked[r, part * ROWS : part * ROWS + ROWS] = upper
        picked[r, HALF + part * ROWS : HALF + part * ROWS + ROWS] = lower


def exact6(a, b, dot):
    a1, a2, a3 = split3(a)
    b1, b2, b3 = split3(b)
    small = dot(a2, b2) + (dot(a1, b3) + dot(a3, b1))
    return small + (dot(a1, b2) + dot(a2, b1)) + dot(a1, b1)


def whiten_slots(picked, inverse, out):
    done = [exact6(p.T, inverse, dot_nt) for p in picked]
    for pair in range(2):
        out[:, pair, :] = jnp.concatenate(done[2 * pair : 2 * pair + 2], axis=1)


def place_samples(incoming, own):
    hot = iota((128, 128), 0) == own
    flag = jnp.where(hot, 1.0, 0.0)
    rank = dot_nn(flag.astype(BF16), earlier())
    total = jnp.zeros((COLS, LANES), F32)
    for pair in range(2):
        top, mid, low = split3(incoming[:, pair, :])
        for half in range(2):
            chosen = jnp.where(rank == float(2 * pair + half), flag, 0.0).astype(BF16)
            got = dot_tn(low, chosen) + dot_tn(mid, chosen) + dot_tn(top, chosen)
            total = total + got[64 * half : 64 * half + 64]
    return total


def position():
    row, y = lax.axis_index("rows"), lax.axis_index("sk")
    return row // 8, (row // 2) % 4, row % 2, y


def device(z, x, c, y):
    return ((z * 4 + x) * 2 + c, y)


def flat(z, x, c, y):
    return ((z * 4 + x) * 2 + c) * 4 + y


def peer(t):
    z, x, c, y = position()
    u = t // 2
    a, b, e = u % 4, (u // 4) % 4, u // 16
    return (z + a + 2 * b + e) % 4, (x + a + b) % 4, (c + t) % 2, (y + a) % 4


def start(src, dst, send_sem, recv_sem, where):
    pltpu.make_async_remote_copy(
        src_ref=src, dst_ref=dst, send_sem=send_sem, recv_sem=recv_sem, device_id=device(*where), device_id_type=MESH
    ).start()


def settle(ref, send_sem, recv_sem):
    whole = pltpu.make_async_remote_copy(
        src_ref=ref, dst_ref=ref, send_sem=send_sem, recv_sem=recv_sem, device_id=device(*peer(1)), device_id_type=MESH
    )
    whole.wait_recv()
    whole.wait_send()


def kernel(
    panel_hbm, signs, sources, offsets, mixed, factor_out, whitened,
    panel, table, send, arrived, back, counts, acc, first_sums, second_sums, picked, slots, incoming,
    out_send, out_recv, back_send, back_recv, one_send, one_recv, two_send, two_recv, slot_send, slot_recv, load_sem,
):
    z, x, c, y = position()
    me = flat(z, x, c, y)
    barrier = pltpu.get_barrier_semaphore()
    loads = [
        pltpu.make_async_copy(panel_hbm.at[pl.ds(8 * g, 8)], panel.at[pl.ds(8 * g, 8)], load_sem.at[g]) for g in range(8)
    ]
    for load in loads:
        load.start()

    def greet(t, carry):
        pl.semaphore_signal(barrier, inc=1, device_id=device(*peer(t)), device_id_type=MESH)
        return carry

    lax.fori_loop(1, 128, greet, 0)
    table[...] = lane_table()
    rows = lambda part: pl.ds(part * ROWS, ROWS)

    def send_out(part):
        def step(t, carry):
            where = peer(t)
            start(send.at[flat(*where), rows(part)], arrived.at[me, rows(part)], out_send.at[part], out_recv.at[part], where)
            return carry

        lax.fori_loop(1, 128, step, 0)
        arrived[me, rows(part)] = send[me, rows(part)]

    def send_back(part, low, high):
        def step(t, carry):
            where = peer(t)
            start(arrived.at[flat(*where), rows(part)], back.at[me, rows(part)], back_send.at[part], back_recv.at[part], where)
            return carry

        lax.fori_loop(low, high, step, 0)

    for part in range(PARTS):
        for g in range(8):
            if (g % 4) * 8 // ROWS == part:
                loads[g].wait()
        local_mix(part, panel, signs, table, send)
        if part == 0:
            pl.semaphore_wait(barrier, 127)
        send_out(part)
    count_rows(sources, offsets, counts, me)
    places = slot_places(sources, offsets, me)
    for part in range(PARTS):
        settle(arrived.at[pl.ds(0, 127), rows(part)], out_send.at[part], out_recv.at[part])
        combine(part, arrived)
        send_back(part, 1, 128 if part < PARTS - 1 else SPLIT)
        back[me, rows(part)] = arrived[me, rows(part)]

    g = gram(arrived, counts, acc)
    mine = c * 4 + y
    first_sums[mine] = jnp.concatenate([g[:32], g[32:]], axis=1)

    def step_one(t, carry):
        where = (z, x, (c + t) % 2, (y + t // 2) % 4)
        start(first_sums.at[mine], first_sums.at[mine], one_send, one_recv, where)
        return carry

    lax.fori_loop(1, 8, step_one, 0)
    send_back(PARTS - 1, SPLIT, 128)
    settle(first_sums.at[pl.ds(0, 7)], one_send, one_recv)
    total = first_sums[0]
    for i in range(1, 8):
        total = total + first_sums[i]
    line = z * 4 + x
    second_sums[line] = total

    def step_two(t, carry):
        where = ((z + t // 4) % 4, (x + t) % 4, c, y)
        start(second_sums.at[line], second_sums.at[line], two_send, two_recv, where)
        return carry

    lax.fori_loop(1, 16, step_two, 0)
    for part in range(PARTS - 1):
        settle(back.at[pl.ds(0, 127), rows(part)], back_send.at[part], back_recv.at[part])
        unpack_part(part, back, mixed, 2.0**-10)
        pick_part(part, mixed, places, picked)
    settle(second_sums.at[pl.ds(0, 15)], two_send, two_recv)
    total = second_sums[0]
    for i in range(1, 16):
        total = total + second_sums[i]
    both = factor(jnp.concatenate([total[:, :64], total[:, 64:]], axis=0) * (2.0**-34))
    factor_out[...] = both[:, :64]

    last = PARTS - 1
    settle(back.at[pl.ds(0, 127), rows(last)], back_send.at[last], back_recv.at[last])
    unpack_part(last, back, mixed, 2.0**-10)
    pick_part(last, mixed, places, picked)
    whiten_slots([picked[r] for r in range(CAP)], both[:, 64:], slots)

    def step_slots(t, carry):
        where = peer(t)
        start(slots.at[flat(*where)], incoming.at[me], slot_send, slot_recv, where)
        return carry

    lax.fori_loop(1, 128, step_slots, 0)
    incoming[me] = slots[me]
    own = sources[pl.ds(me, 1), :]
    settle(incoming.at[pl.ds(0, 127)], slot_send, slot_recv)
    whitened[...] = place_samples(incoming, own)


def local(panel, signs, sample_device, sample_offset):
    shape = lambda *dims: jax.ShapeDtypeStruct(dims, F32)
    vmem = pl.BlockSpec(memory_space=pltpu.VMEM)
    dma = pltpu.SemaphoreType.DMA
    return pl.pallas_call(
        kernel,
        out_shape=(shape(64, 8192), shape(64, 64), shape(64, 128)),
        in_specs=[pl.BlockSpec(memory_space=pl.ANY), vmem, vmem, vmem],
        out_specs=(vmem, vmem, vmem),
        scratch_shapes=[
            pltpu.VMEM((64, 8192), F32),
            pltpu.VMEM((256, 256), BF16),
            pltpu.VMEM((DEVS, HALF, LANES), F32),
            pltpu.VMEM((DEVS, HALF, LANES), F32),
            pltpu.VMEM((DEVS, HALF, LANES), F32),
            pltpu.VMEM((64, 128), F32),
            pltpu.VMEM((192, 192), F32),
            pltpu.VMEM((8, 32, 128), F32),
            pltpu.VMEM((16, 32, 128), F32),
            pltpu.VMEM((CAP, 64, 128), F32),
            pltpu.VMEM((DEVS, 2, LANES), F32),
            pltpu.VMEM((DEVS, 2, LANES), F32),
            dma((PARTS,)), dma((PARTS,)), dma((PARTS,)), dma((PARTS,)),
            dma, dma, dma, dma, dma, dma, dma((8,)),
        ],
        compiler_params=pltpu.CompilerParams(collective_id=0, has_side_effects=True, vmem_limit_bytes=56 << 20),
    )(panel, signs.reshape(1, -1), sample_device.reshape(128, 128), sample_offset.reshape(128, 128))


def solution(mesh):
    return jax.shard_map(
        local,
        mesh=mesh,
        in_specs=(P(None, AXES), P(AXES), P(), P()),
        out_specs=(P(None, AXES), P(), P(None, AXES)),
        check_vma=False,
    )
```

```python
import jax
import jax.numpy as jnp
from jax import lax
from jax.experimental import pallas as pl
from jax.experimental.pallas import tpu as pltpu
from jax.sharding import PartitionSpec as P

F32, BF16, I32 = jnp.float32, jnp.bfloat16, jnp.int32
AXES = ("rows", "sk")
DEVS, COLS, HALF, LANES, CAP = 128, 64, 32, 128, 4


def split3(x):
    top = x.astype(BF16)
    rest = x - top.astype(F32)
    mid = rest.astype(BF16)
    low = (rest - mid.astype(F32)).astype(BF16)
    return top, mid, low


def dot_nn(a, b):
    return lax.dot_general(a, b, (((1,), (0,)), ((), ())), preferred_element_type=F32)


def dot_nt(a, b):
    return lax.dot_general(a, b, (((1,), (1,)), ((), ())), preferred_element_type=F32)


def dot_tn(a, b):
    return lax.dot_general(a, b, (((0,), (0,)), ((), ())), preferred_element_type=F32)


def iota(shape, dim):
    return lax.broadcasted_iota(I32, shape, dim)


def butterflies(values):
    size, step = len(values), 1
    while step < size:
        nxt = list(values)
        for i in range(size):
            if not i & step:
                nxt[i] = values[i] + values[i + step]
                nxt[i + step] = values[i] - values[i + step]
        values, step = nxt, step * 2
    return values


def lane_table():
    k, n = iota((256, 256), 0), iota((256, 256), 1)
    bits = jnp.bitwise_and(k % 128, (n // 128) * 64 + n % 64)
    for shift in (4, 2, 1):
        bits = jnp.bitwise_xor(bits, lax.shift_right_logical(bits, shift))
    sign = 1.0 - 2.0 * jnp.bitwise_and(bits, 1).astype(F32)
    return jnp.where(k // 128 == (n % 128) // 64, sign, 0.0).astype(BF16)
HELD, AHEAD = 105, 50


PARTS = 2
ROWS = HALF // PARTS
MESH = pl.DeviceIdType.MESH


def local_mix(part, panel, signs, table, send):
    at_rows = pl.ds(part * ROWS, ROWS)

    def first(high, carry):
        at = pl.ds(pl.multiple_of(high * 1024, 1024), 1024)
        sign = signs[:, at].astype(F32)
        upper = panel[part * ROWS : part * ROWS + ROWS, at] * sign
        lower = panel[HALF + part * ROWS : HALF + part * ROWS + ROWS, at] * sign
        lhs = jnp.concatenate(
            [
                jnp.concatenate([upper[:, 128 * b : 128 * b + 128], lower[:, 128 * b : 128 * b + 128]], axis=1)
                for b in range(8)
            ],
            axis=0,
        )
        weights = table[...]
        top, mid, low = split3(lhs)
        out = dot_nn(low, weights) + dot_nn(mid, weights) + dot_nn(top, weights)
        done = butterflies([out[ROWS * b : ROWS * b + ROWS] for b in range(8)])
        for b in range(8):
            send[16 * high + 2 * b, at_rows] = done[b][:, :128]
            send[16 * high + 2 * b + 1, at_rows] = done[b][:, 128:]
        return carry

    lax.fori_loop(0, 8, first, 0)

    def second(low, carry):
        done = butterflies([send[16 * high + low, at_rows] for high in range(8)])
        for high in range(8):
            send[16 * high + low, at_rows] = done[high]
        return carry

    lax.fori_loop(0, 16, second, 0)


def combine(part, data):
    def first(i, carry):
        high, group = i // (ROWS // 8), i % (ROWS // 8)
        at = pl.ds(pl.multiple_of(part * ROWS + group * 8, 8), 8)
        done = butterflies([data[16 * high + low, at] for low in range(16)])
        for low in range(16):
            data[16 * high + low, at] = done[low]
        return carry

    lax.fori_loop(0, 8 * (ROWS // 8), first, 0)
    at_rows = pl.ds(part * ROWS, ROWS)

    def second(low, carry):
        done = butterflies([data[16 * high + low, at_rows] for high in range(8)])
        for high in range(8):
            data[16 * high + low, at_rows] = done[high]
        return carry

    lax.fori_loop(0, 16, second, 0)


def count_rows(sources, offsets, counts, me):
    counts[...] = jnp.zeros_like(counts)

    def step(i, carry):
        at = pl.ds(pl.multiple_of(i * 8, 8), 8)
        src8, rel8 = sources[at, :], offsets[at, :] - me * 64
        inside = jnp.logical_and(rel8 >= 0, rel8 < 64)
        lane8 = jnp.where(inside, rel8 + jnp.where(src8 >= 64, 64, 0), -1)
        q8 = jnp.bitwise_and(src8, 63)
        total = counts[...]
        for pair in range(4):
            q = jnp.concatenate([q8[2 * pair : 2 * pair + 1], q8[2 * pair + 1 : 2 * pair + 2]], axis=1)
            lane = jnp.concatenate([lane8[2 * pair : 2 * pair + 1], lane8[2 * pair + 1 : 2 * pair + 2]], axis=1)
            left = jnp.where(iota((64, 256), 0) == q, 1.0, 0.0).astype(BF16)
            right = jnp.where(iota((128, 256), 0) == lane, 1.0, 0.0).astype(BF16)
            total = total + dot_nt(left, right)
        counts[...] = total
        return carry

    lax.fori_loop(0, 16, step, 0)
    counts[...] = jnp.sqrt(counts[...])


def weighted_parts(part, data, roots, i):
    left = iota((ROWS, LANES), 1) < 64
    pieces = []
    for q in (2 * i, 2 * i + 1):
        one, two = data[q, pl.ds(part * ROWS, ROWS)], data[q + 64, pl.ds(part * ROWS, ROWS)]
        upper = jnp.where(left, one, pltpu.roll(two, 64, 1))
        lower = jnp.where(left, pltpu.roll(one, 64, 1), two)
        pieces.append(jnp.concatenate([upper, lower], axis=0) * roots[pl.ds(q, 1), :])
    return jnp.concatenate(split3(jnp.concatenate(pieces, axis=1)), axis=0)


def gram_first(data, roots, parts, acc):
    acc[...] = jnp.zeros_like(acc)

    def step(i, carry):
        total = acc[...]
        for k in range(4):
            own = weighted_parts(0, data, roots, 4 * i + k)
            parts[4 * i + k] = own
            total = total + dot_nt(own, own)
        acc[...] = total
        return carry

    lax.fori_loop(0, 8, step, 0)


def gram_second(data, roots, parts, acc):
    acc[...] = jnp.zeros_like(acc)

    def step(i, carry):
        total = acc[...]
        for k in range(4):
            own = weighted_parts(1, data, roots, 4 * i + k)
            total = total + dot_nt(jnp.concatenate([parts[4 * i + k], own], axis=0), own)
        acc[...] = total
        return carry

    lax.fori_loop(0, 8, step, 0)


def merge_parts(acc, row):
    block = lambda i, j: acc[row + 32 * i : row + 32 * i + 32, 32 * j : 32 * j + 32]
    small = block(2, 2) + (block(1, 2) + block(2, 1))
    small = small + (block(0, 2) + block(2, 0)) + block(1, 1)
    return small + (block(0, 1) + block(1, 0)) + block(0, 0)


def gram(first, second):
    same, cross, last = merge_parts(first, 0), merge_parts(second, 0), merge_parts(second, 96)
    g = jnp.concatenate(
        [jnp.concatenate([same, cross], axis=1), jnp.concatenate([cross.T, last], axis=1)], axis=0
    )
    swap = lambda m, dim: jnp.concatenate(
        [lax.slice_in_dim(m, at, at + 16, axis=dim) for at in (0, 32, 16, 48)], axis=dim
    )
    g = swap(swap(g, 0), 1)
    return jnp.concatenate([g[:32], g[32:]], axis=1)


def factor(g):
    sub, lane = iota((COLS, LANES), 0), iota((COLS, LANES), 1)
    m = jnp.concatenate([g, jnp.where(sub == lane, 1.0, 0.0)[:, :64]], axis=1)
    subs = iota((COLS, 1), 0)
    for j in range(COLS):
        pivot_row = m[j : j + 1, :]
        inverse = 1.0 / m[j : j + 1, j : j + 1]
        lead = jnp.where(subs > j, m[:, j : j + 1] * inverse, 0.0)
        m = m - lead * pivot_row
    diagonal = jnp.sum(jnp.where(sub == lane, m, 0.0), axis=1, keepdims=True)
    scaled = m / jnp.sqrt(diagonal)
    return jnp.where(jnp.logical_or(lane >= sub, lane >= 64), scaled, 0.0)


def earlier():
    return jnp.where(iota((128, 128), 0) < iota((128, 128), 1), 1.0, 0.0).astype(BF16)


def slot_places(sources, offsets, me):
    mine = sources[...] == me
    rank = dot_nn(jnp.where(mine, 1.0, 0.0).astype(BF16), earlier())
    high = (offsets[...] // 128).astype(F32)
    low = (offsets[...] % 128).astype(F32)
    ones = jnp.ones((8, 128), BF16)
    places = []
    for r in range(CAP):
        chosen = jnp.logical_and(mine, rank == float(r))
        places.append(
            tuple(dot_nt(ones, jnp.where(chosen, v, 0.0).astype(BF16)).astype(I32) for v in (high, low))
        )
    return places


def unpack_part(part, back, mixed, scale):
    left = iota((ROWS, LANES), 1) < 64

    def step(i, carry):
        for k in range(8):
            b = 8 * i + k
            at = pl.ds(pl.multiple_of(b * 128, 128), 128)
            one, two = back[2 * b, pl.ds(part * ROWS, ROWS)], back[2 * b + 1, pl.ds(part * ROWS, ROWS)]
            upper = jnp.where(left, one, pltpu.roll(two, 64, 1))
            lower = jnp.where(left, pltpu.roll(one, 64, 1), two)
            mixed[part * ROWS : part * ROWS + ROWS, at] = upper * scale
            mixed[HALF + part * ROWS : HALF + part * ROWS + ROWS, at] = lower * scale
        return carry

    lax.fori_loop(0, 8, step, 0)


def pick_part(part, mixed, places, picked):
    bases = [half + part * ROWS + 8 * k for half in (0, HALF) for k in range(ROWS // 8)]
    for r, (high, low) in enumerate(places):

        def step(i, found):
            for k in range(16):
                b = 16 * i + k
                at = pl.ds(pl.multiple_of(b * 128, 128), 128)
                here = high == b
                found = tuple(
                    jnp.where(
                        here,
                        jnp.take_along_axis(mixed[base : base + 8, at], low, axis=1, mode="promise_in_bounds"),
                        old,
                    )
                    for base, old in zip(bases, found)
                )
            return found

        done = lax.fori_loop(0, 4, step, tuple(jnp.zeros((8, LANES), F32) for _ in bases))
        for base, value in zip(bases, done):
            picked[r, base : base + 8] = value


def exact6(a, b, dot):
    a1, a2, a3 = split3(a)
    b1, b2, b3 = split3(b)
    small = dot(a2, b2) + (dot(a1, b3) + dot(a3, b1))
    return small + (dot(a1, b2) + dot(a2, b1)) + dot(a1, b1)


def whiten_slots(picked, inverse, out):
    done = [exact6(p.T, inverse, dot_nt) for p in picked]
    for pair in range(2):
        out[:, :, pair, :] = jnp.concatenate(done[2 * pair : 2 * pair + 2], axis=1).reshape(16, 8, LANES)


def place_samples(incoming, own):
    hot = iota((128, 128), 0) == own
    flag = jnp.where(hot, 1.0, 0.0)
    rank = dot_nn(flag.astype(BF16), earlier())
    total = jnp.zeros((COLS, LANES), F32)
    for pair in range(2):
        top, mid, low = split3(incoming[:, :, pair, :].reshape(DEVS, LANES))
        for half in range(2):
            chosen = jnp.where(rank == float(2 * pair + half), flag, 0.0).astype(BF16)
            got = dot_tn(low, chosen) + dot_tn(mid, chosen) + dot_tn(top, chosen)
            total = total + got[64 * half : 64 * half + 64]
    return total


def position():
    row, y = lax.axis_index("rows"), lax.axis_index("sk")
    return row // 8, (row // 2) % 4, row % 2, y


def device(z, x, c, y):
    return ((z * 4 + x) * 2 + c, y)


def flat(z, x, c, y):
    return ((z * 4 + x) * 2 + c) * 4 + y


def in_line(t):
    z, x, c, y = position()
    return z, x, (c + t) % 2, (y + t // 2) % 4


def in_plane(t):
    z, x, c, y = position()
    return (z + t // 4 + t) % 4, (x + t) % 4, c, y


def elsewhere(i):
    z, x, _, _ = in_plane(1 + i % 15)
    _, _, c, y = in_line(1 + i % 7)
    return z, x, c, y


def run(low, high, step):
    whole = (high - low) // 7

    def several(i, carry):
        for k in range(7):
            step(low + 7 * i + k, 0)
        return carry

    lax.fori_loop(0, whole, several, 0)
    for t in range(low + 7 * whole, high):
        step(t, 0)


GROUPS = ((in_line, 1, 8), (in_plane, 1, 16), (elsewhere, 0, 105))


def start(src, dst, send_sem, recv_sem, where):
    pltpu.make_async_remote_copy(
        src_ref=src, dst_ref=dst, send_sem=send_sem, recv_sem=recv_sem, device_id=device(*where), device_id_type=MESH
    ).start()


def settle(ref, send_sem, recv_sem):
    whole = pltpu.make_async_remote_copy(
        src_ref=ref, dst_ref=ref, send_sem=send_sem, recv_sem=recv_sem, device_id=device(*in_line(1)), device_id_type=MESH
    )
    whole.wait_recv()
    whole.wait_send()


def kernel(
    panel_hbm, signs_hbm, sources_hbm, offsets_hbm, mixed, factor_out, whitened,
    panel, signs, sources, offsets, table, send, arrived, back, counts, parts, acc, acc2, first_sums, second_sums, picked, slots, relay, incoming,
    out_send, out_recv, back_send, back_recv, one_send, one_recv, two_send, two_recv,
    line_send, line_recv, plane_send, plane_recv, load_sem, ready,
):
    z, x, c, y = position()
    me = flat(z, x, c, y)
    barrier = pltpu.get_barrier_semaphore()
    loads = [
        pltpu.make_async_copy(panel_hbm.at[pl.ds(8 * g, 8)], panel.at[pl.ds(8 * g, 8)], load_sem.at[g]) for g in range(8)
    ]
    tables = [
        pltpu.make_async_copy(src, dst, load_sem.at[8 + i])
        for i, (src, dst) in enumerate(((signs_hbm, signs), (sources_hbm, sources), (offsets_hbm, offsets)))
    ]
    for load in tables[:1] + loads + tables[1:]:
        load.start()

    def signal_all(sem, peers, count):
        def step(t, carry):
            pl.semaphore_signal(sem, inc=1, device_id=device(*peers(t)), device_id_type=MESH)
            return carry

        lax.fori_loop(1, count, step, 0)

    signal_all(barrier, in_line, 8)
    signal_all(barrier, in_plane, 16)
    table[...] = lane_table()
    rows = lambda part: pl.ds(part * ROWS, ROWS)

    def send_out(part, groups):
        for group, low, high in groups:

            def step(t, carry):
                where = group(t)
                start(send.at[flat(*where), rows(part)], arrived.at[me, rows(part)], out_send.at[part], out_recv.at[part], where)
                return carry

            run(low, high, step)

    def send_back(part, groups):
        for group, low, high in groups:

            def step(t, carry):
                where = group(t)
                start(arrived.at[flat(*where), rows(part)], back.at[me, rows(part)], back_send.at[part], back_recv.at[part], where)
                return carry

            run(low, high, step)

    tables[0].wait()
    for part in range(PARTS):
        for g in range(8):
            if (g % 4) * 8 // ROWS == part:
                loads[g].wait()
        local_mix(part, panel, signs, table, send)
        if part == 0:
            pl.semaphore_wait(barrier, 22)
            signal_all(ready, in_plane, 16)
        send_out(part, GROUPS[:2])
    pl.semaphore_wait(ready, 15)
    for part in range(PARTS):
        send_out(part, GROUPS[2:])
        arrived[me, rows(part)] = send[me, rows(part)]
    tables[1].wait()
    tables[2].wait()
    count_rows(sources, offsets, counts, me)
    places = slot_places(sources, offsets, me)
    for part in range(PARTS):
        settle(arrived.at[pl.ds(0, 127), rows(part)], out_send.at[part], out_recv.at[part])
        combine(part, arrived)
        if part == 0:
            send_back(0, ((elsewhere, 0, HELD),))
        back[me, rows(part)] = arrived[me, rows(part)]
        if part == 0:
            gram_first(arrived, counts, parts, acc)
    gram_second(arrived, counts, parts, acc2)
    line, plane = c * 4 + y, z * 4 + x
    first_sums[line] = gram(acc, acc2)

    def send_sums(sums, at, peers, count, send_sem, recv_sem):
        def step(t, carry):
            start(sums.at[at], sums.at[at], send_sem, recv_sem, peers(t))
            return carry

        lax.fori_loop(1, count, step, 0)

    send_sums(first_sums, line, in_line, 8, one_send, one_recv)
    send_back(0, ((elsewhere, HELD, 105),) + GROUPS[:2])
    send_back(1, ((elsewhere, 0, AHEAD),))
    settle(first_sums.at[pl.ds(0, 7)], one_send, one_recv)
    total = first_sums[0]
    for i in range(1, 8):
        total = total + first_sums[i]
    second_sums[plane] = total
    send_sums(second_sums, plane, in_plane, 16, two_send, two_recv)
    send_back(1, ((elsewhere, AHEAD, 105),) + GROUPS[:2])
    for part in range(PARTS - 1):
        settle(back.at[pl.ds(0, 127), rows(part)], back_send.at[part], back_recv.at[part])
        unpack_part(part, back, mixed, 2.0**-10)
        pick_part(part, mixed, places, picked)
    settle(second_sums.at[pl.ds(0, 15)], two_send, two_recv)
    total = second_sums[0]
    for i in range(1, 16):
        total = total + second_sums[i]
    both = factor(jnp.concatenate([total[:, :64], total[:, 64:]], axis=0) * (2.0**-34))
    factor_out[...] = both[:, :64]

    last = PARTS - 1
    settle(back.at[pl.ds(0, 127), rows(last)], back_send.at[last], back_recv.at[last])
    unpack_part(last, back, mixed, 2.0**-10)
    pick_part(last, mixed, places, picked)
    whiten_slots([picked[r] for r in range(CAP)], both[:, 64:], slots)

    def step_line(t, carry):
        _, _, pc, py = where = in_line(t)
        start(slots.at[:, pc * 4 + py], relay.at[line], line_send, line_recv, where)
        return carry

    lax.fori_loop(1, 8, step_line, 0)
    relay[line] = slots[:, line]
    own = sources[pl.ds(me, 1), :]
    settle(relay.at[pl.ds(0, 7)], line_send, line_recv)

    def step_plane(t, carry):
        pz, px, _, _ = where = in_plane(t)
        start(relay.at[:, pz * 4 + px], incoming.at[plane], plane_send, plane_recv, where)
        return carry

    lax.fori_loop(1, 16, step_plane, 0)
    incoming[plane] = relay[:, plane]
    settle(incoming.at[pl.ds(0, 15)], plane_send, plane_recv)
    whitened[...] = place_samples(incoming, own)


def pass_on(mixed_in, factor_in, whitened_in, mixed, factor_out, whitened, sems):
    pairs = [(mixed_in.at[pl.ds(8 * g, 8)], mixed.at[pl.ds(8 * g, 8)]) for g in range(8)]
    pairs += [(factor_in, factor_out), (whitened_in, whitened)]
    copies = [pltpu.make_async_copy(src, dst, sems.at[i]) for i, (src, dst) in enumerate(pairs)]
    for copy in copies:
        copy.start()
    for copy in copies:
        copy.wait()


def local(panel, signs, sample_device, sample_offset):
    shape = lambda *dims: jax.ShapeDtypeStruct(dims, F32)
    vmem = pl.BlockSpec(memory_space=pltpu.VMEM)
    dma = pltpu.SemaphoreType.DMA
    made = pl.pallas_call(
        kernel,
        out_shape=(shape(64, 8192), shape(64, 64), shape(64, 128)),
        in_specs=[pl.BlockSpec(memory_space=pltpu.HBM)] * 4,
        out_specs=(vmem, vmem, vmem),
        scratch_shapes=[
            pltpu.VMEM((64, 8192), F32),
            pltpu.VMEM((1, 8192), I32),
            pltpu.VMEM((128, 128), I32),
            pltpu.VMEM((128, 128), I32),
            pltpu.VMEM((256, 256), BF16),
            pltpu.VMEM((DEVS, HALF, LANES), F32),
            pltpu.VMEM((DEVS, HALF, LANES), F32),
            pltpu.VMEM((DEVS, HALF, LANES), F32),
            pltpu.VMEM((64, 128), F32),
            pltpu.VMEM((32, 96, 256), BF16),
            pltpu.VMEM((96, 96), F32),
            pltpu.VMEM((192, 96), F32),
            pltpu.VMEM((8, 32, 128), F32),
            pltpu.VMEM((16, 32, 128), F32),
            pltpu.VMEM((CAP, 64, 128), F32),
            pltpu.VMEM((16, 8, 2, LANES), F32),
            pltpu.VMEM((8, 16, 2, LANES), F32),
            pltpu.VMEM((16, 8, 2, LANES), F32),
            dma((PARTS,)), dma((PARTS,)), dma((PARTS,)), dma((PARTS,)),
            dma, dma, dma, dma, dma, dma, dma, dma, dma((11,)), pltpu.SemaphoreType.REGULAR,
        ],
        compiler_params=pltpu.CompilerParams(collective_id=0, has_side_effects=True, vmem_limit_bytes=20 << 20),
    )(*(pltpu.with_memory_space_constraint(v, pltpu.HBM) for v in (panel, signs.reshape(1, -1), sample_device.reshape(128, 128), sample_offset.reshape(128, 128))))
    anywhere = pl.BlockSpec(memory_space=pl.ANY)
    return pl.pallas_call(
        pass_on,
        out_shape=(shape(64, 8192), shape(64, 64), shape(64, 128)),
        in_specs=[vmem, vmem, vmem],
        out_specs=(anywhere, anywhere, anywhere),
        scratch_shapes=[dma((10,))],
        compiler_params=pltpu.CompilerParams(vmem_limit_bytes=8 << 20),
    )(*made)


def solution(mesh):
    return jax.shard_map(
        local,
        mesh=mesh,
        in_specs=(P(None, AXES), P(AXES), P(), P()),
        out_specs=(P(None, AXES), P(), P(None, AXES)),
        check_vma=False,
    )
```

```python
import jax
import jax.numpy as jnp
from jax import lax
from jax.experimental import pallas as pl
from jax.experimental.pallas import tpu as pltpu
from jax.sharding import PartitionSpec as P

F32, BF16, I32 = jnp.float32, jnp.bfloat16, jnp.int32
AXES = ("rows", "sk")
DEVS, COLS, HALF, LANES, CAP = 128, 64, 32, 128, 4


def split3(x):
    top = x.astype(BF16)
    rest = x - top.astype(F32)
    mid = rest.astype(BF16)
    low = (rest - mid.astype(F32)).astype(BF16)
    return top, mid, low


def dot_nn(a, b):
    return lax.dot_general(a, b, (((1,), (0,)), ((), ())), preferred_element_type=F32)


def dot_nt(a, b):
    return lax.dot_general(a, b, (((1,), (1,)), ((), ())), preferred_element_type=F32)


def dot_tn(a, b):
    return lax.dot_general(a, b, (((0,), (0,)), ((), ())), preferred_element_type=F32)


def iota(shape, dim):
    return lax.broadcasted_iota(I32, shape, dim)


def butterflies(values):
    size, step = len(values), 1
    while step < size:
        nxt = list(values)
        for i in range(size):
            if not i & step:
                nxt[i] = values[i] + values[i + step]
                nxt[i + step] = values[i] - values[i + step]
        values, step = nxt, step * 2
    return values


def lane_table():
    k, n = iota((256, 256), 0), iota((256, 256), 1)
    bits = jnp.bitwise_and(k % 128, (n // 128) * 64 + n % 64)
    for shift in (4, 2, 1):
        bits = jnp.bitwise_xor(bits, lax.shift_right_logical(bits, shift))
    sign = 1.0 - 2.0 * jnp.bitwise_and(bits, 1).astype(F32)
    return jnp.where(k // 128 == (n % 128) // 64, sign, 0.0).astype(BF16)
MIDDLE = 24


PARTS = 2
ROWS = HALF // PARTS
MESH = pl.DeviceIdType.MESH


def local_mix(part, panel, signs, table, send):
    at_rows = pl.ds(part * ROWS, ROWS)

    def first(high, carry):
        at = pl.ds(pl.multiple_of(high * 1024, 1024), 1024)
        sign = signs[:, at].astype(F32)
        upper = panel[part * ROWS : part * ROWS + ROWS, at] * sign
        lower = panel[HALF + part * ROWS : HALF + part * ROWS + ROWS, at] * sign
        lhs = jnp.concatenate(
            [
                jnp.concatenate([upper[:, 128 * b : 128 * b + 128], lower[:, 128 * b : 128 * b + 128]], axis=1)
                for b in range(8)
            ],
            axis=0,
        )
        weights = table[...]
        top, mid, low = split3(lhs)
        out = dot_nn(low, weights) + dot_nn(mid, weights) + dot_nn(top, weights)
        done = butterflies([out[ROWS * b : ROWS * b + ROWS] for b in range(8)])
        for b in range(8):
            send[16 * high + 2 * b, at_rows] = done[b][:, :128]
            send[16 * high + 2 * b + 1, at_rows] = done[b][:, 128:]
        return carry

    lax.fori_loop(0, 8, first, 0)

    def second(low, carry):
        done = butterflies([send[16 * high + low, at_rows] for high in range(8)])
        for high in range(8):
            send[16 * high + low, at_rows] = done[high]
        return carry

    lax.fori_loop(0, 16, second, 0)


def combine(part, data):
    def first(i, carry):
        high, group = i // (ROWS // 8), i % (ROWS // 8)
        at = pl.ds(pl.multiple_of(part * ROWS + group * 8, 8), 8)
        done = butterflies([data[16 * high + low, at] for low in range(16)])
        for low in range(16):
            data[16 * high + low, at] = done[low]
        return carry

    lax.fori_loop(0, 8 * (ROWS // 8), first, 0)
    at_rows = pl.ds(part * ROWS, ROWS)

    def second(low, carry):
        done = butterflies([data[16 * high + low, at_rows] for high in range(8)])
        for high in range(8):
            data[16 * high + low, at_rows] = done[high]
        return carry

    lax.fori_loop(0, 16, second, 0)


def count_rows(sources, offsets, counts, me):
    counts[...] = jnp.zeros_like(counts)

    def step(i, carry):
        at = pl.ds(pl.multiple_of(i * 8, 8), 8)
        src8, rel8 = sources[at, :], offsets[at, :] - me * 64
        inside = jnp.logical_and(rel8 >= 0, rel8 < 64)
        lane8 = jnp.where(inside, rel8 + jnp.where(src8 >= 64, 64, 0), -1)
        q8 = jnp.bitwise_and(src8, 63)
        total = counts[...]
        for pair in range(4):
            q = jnp.concatenate([q8[2 * pair : 2 * pair + 1], q8[2 * pair + 1 : 2 * pair + 2]], axis=1)
            lane = jnp.concatenate([lane8[2 * pair : 2 * pair + 1], lane8[2 * pair + 1 : 2 * pair + 2]], axis=1)
            left = jnp.where(iota((64, 256), 0) == q, 1.0, 0.0).astype(BF16)
            right = jnp.where(iota((128, 256), 0) == lane, 1.0, 0.0).astype(BF16)
            total = total + dot_nt(left, right)
        counts[...] = total
        return carry

    lax.fori_loop(0, 16, step, 0)
    counts[...] = jnp.sqrt(counts[...])


def weighted_parts(part, data, roots, i):
    left = iota((ROWS, LANES), 1) < 64
    pieces = []
    for q in (2 * i, 2 * i + 1):
        one, two = data[q, pl.ds(part * ROWS, ROWS)], data[q + 64, pl.ds(part * ROWS, ROWS)]
        upper = jnp.where(left, one, pltpu.roll(two, 64, 1))
        lower = jnp.where(left, pltpu.roll(one, 64, 1), two)
        pieces.append(jnp.concatenate([upper, lower], axis=0) * roots[pl.ds(q, 1), :])
    return jnp.concatenate(split3(jnp.concatenate(pieces, axis=1)), axis=0)


def gram_first(data, roots, parts, acc):
    acc[...] = jnp.zeros_like(acc)

    def step(i, carry):
        total = acc[...]
        for k in range(4):
            own = weighted_parts(0, data, roots, 4 * i + k)
            parts[4 * i + k] = own
            total = total + dot_nt(own, own)
        acc[...] = total
        return carry

    lax.fori_loop(0, 8, step, 0)


def gram_second(data, roots, parts, acc):
    acc[...] = jnp.zeros_like(acc)

    def step(i, carry):
        total = acc[...]
        for k in range(4):
            own = weighted_parts(1, data, roots, 4 * i + k)
            total = total + dot_nt(jnp.concatenate([parts[4 * i + k], own], axis=0), own)
        acc[...] = total
        return carry

    lax.fori_loop(0, 8, step, 0)


def merge_parts(acc, row):
    block = lambda i, j: acc[row + 32 * i : row + 32 * i + 32, 32 * j : 32 * j + 32]
    small = block(2, 2) + (block(1, 2) + block(2, 1))
    small = small + (block(0, 2) + block(2, 0)) + block(1, 1)
    return small + (block(0, 1) + block(1, 0)) + block(0, 0)


def gram(first, second):
    same, cross, last = merge_parts(first, 0), merge_parts(second, 0), merge_parts(second, 96)
    g = jnp.concatenate(
        [jnp.concatenate([same, cross], axis=1), jnp.concatenate([cross.T, last], axis=1)], axis=0
    )
    swap = lambda m, dim: jnp.concatenate(
        [lax.slice_in_dim(m, at, at + 16, axis=dim) for at in (0, 32, 16, 48)], axis=dim
    )
    g = swap(swap(g, 0), 1)
    return jnp.concatenate([g[:32], g[32:]], axis=1)


def bordered(g):
    return jnp.concatenate([g, jnp.where(iota((COLS, 64), 0) == iota((COLS, 64), 1), 1.0, 0.0)], axis=1)


def eliminate(m, low, high):
    subs = iota((COLS, 1), 0)
    for j in range(low, high):
        pivot_row = m[j : j + 1, :]
        inverse = 1.0 / m[j : j + 1, j : j + 1]
        lead = jnp.where(subs > j, m[:, j : j + 1] * inverse, 0.0)
        m = m - lead * pivot_row
    return m


def factors(m):
    sub, lane = iota((COLS, LANES), 0), iota((COLS, LANES), 1)
    diagonal = jnp.sum(jnp.where(sub == lane, m, 0.0), axis=1, keepdims=True)
    scaled = m / jnp.sqrt(diagonal)
    return jnp.where(jnp.logical_or(lane >= sub, lane >= 64), scaled, 0.0)


def earlier():
    return jnp.where(iota((128, 128), 0) < iota((128, 128), 1), 1.0, 0.0).astype(BF16)


def slot_places(sources, offsets, me):
    mine = sources[...] == me
    rank = dot_nn(jnp.where(mine, 1.0, 0.0).astype(BF16), earlier())
    high = (offsets[...] // 128).astype(F32)
    low = (offsets[...] % 128).astype(F32)
    ones = jnp.ones((8, 128), BF16)
    places = []
    for r in range(CAP):
        chosen = jnp.logical_and(mine, rank == float(r))
        places.append(
            tuple(dot_nt(ones, jnp.where(chosen, v, 0.0).astype(BF16)).astype(I32) for v in (high, low))
        )
    return places


def unpack_part(part, back, mixed, scale):
    left = iota((ROWS, LANES), 1) < 64

    def step(i, carry):
        for k in range(8):
            b = 8 * i + k
            at = pl.ds(pl.multiple_of(b * 128, 128), 128)
            one, two = back[2 * b, pl.ds(part * ROWS, ROWS)], back[2 * b + 1, pl.ds(part * ROWS, ROWS)]
            upper = jnp.where(left, one, pltpu.roll(two, 64, 1))
            lower = jnp.where(left, pltpu.roll(one, 64, 1), two)
            mixed[part * ROWS : part * ROWS + ROWS, at] = upper * scale
            mixed[HALF + part * ROWS : HALF + part * ROWS + ROWS, at] = lower * scale
        return carry

    lax.fori_loop(0, 8, step, 0)


def pick_part(part, mixed, places, picked):
    bases = [half + part * ROWS + 8 * k for half in (0, HALF) for k in range(ROWS // 8)]
    for r, (high, low) in enumerate(places):

        def step(i, found):
            for k in range(16):
                b = 16 * i + k
                at = pl.ds(pl.multiple_of(b * 128, 128), 128)
                here = high == b
                found = tuple(
                    jnp.where(
                        here,
                        jnp.take_along_axis(mixed[base : base + 8, at], low, axis=1, mode="promise_in_bounds"),
                        old,
                    )
                    for base, old in zip(bases, found)
                )
            return found

        done = lax.fori_loop(0, 4, step, tuple(jnp.zeros((8, LANES), F32) for _ in bases))
        for base, value in zip(bases, done):
            picked[r, base : base + 8] = value


def exact6(a, b, dot):
    a1, a2, a3 = split3(a)
    b1, b2, b3 = split3(b)
    small = dot(a2, b2) + (dot(a1, b3) + dot(a3, b1))
    return small + (dot(a1, b2) + dot(a2, b1)) + dot(a1, b1)


def pack_slots(picked, out):
    for pair in range(2):
        both = jnp.concatenate([picked[2 * pair].T, picked[2 * pair + 1].T], axis=1)
        out[:, :, pair, :] = both.reshape(16, 8, LANES)


def place_samples(incoming, own):
    hot = iota((128, 128), 0) == own
    flag = jnp.where(hot, 1.0, 0.0)
    rank = dot_nn(flag.astype(BF16), earlier())
    total = jnp.zeros((COLS, LANES), F32)
    for pair in range(2):
        top, mid, low = split3(incoming[:, :, pair, :].reshape(DEVS, LANES))
        for half in range(2):
            chosen = jnp.where(rank == float(2 * pair + half), flag, 0.0).astype(BF16)
            got = dot_tn(low, chosen) + dot_tn(mid, chosen) + dot_tn(top, chosen)
            total = total + got[64 * half : 64 * half + 64]
    return total


def position():
    row, y = lax.axis_index("rows"), lax.axis_index("sk")
    return row // 8, (row // 2) % 4, row % 2, y


def device(z, x, c, y):
    return ((z * 4 + x) * 2 + c, y)


def flat(z, x, c, y):
    return ((z * 4 + x) * 2 + c) * 4 + y


def in_line(t):
    z, x, c, y = position()
    return z, x, (c + t) % 2, (y + t // 2) % 4


def in_plane(t):
    z, x, c, y = position()
    return (z + t // 4 + t) % 4, (x + t) % 4, c, y


def elsewhere(i):
    z, x, _, _ = in_plane(1 + i % 15)
    _, _, c, y = in_line(1 + i % 7)
    return z, x, c, y


def run(low, high, step):
    whole = (high - low) // 7

    def several(i, carry):
        for k in range(7):
            step(low + 7 * i + k, 0)
        return carry

    lax.fori_loop(0, whole, several, 0)
    for t in range(low + 7 * whole, high):
        step(t, 0)


GROUPS = ((in_line, 1, 8), (in_plane, 1, 16), (elsewhere, 0, 105))


def start(src, dst, send_sem, recv_sem, where):
    pltpu.make_async_remote_copy(
        src_ref=src, dst_ref=dst, send_sem=send_sem, recv_sem=recv_sem, device_id=device(*where), device_id_type=MESH
    ).start()


def settle(ref, send_sem, recv_sem):
    whole = pltpu.make_async_remote_copy(
        src_ref=ref, dst_ref=ref, send_sem=send_sem, recv_sem=recv_sem, device_id=device(*in_line(1)), device_id_type=MESH
    )
    whole.wait_recv()
    whole.wait_send()


def kernel(
    panel_hbm, signs_hbm, sources_hbm, offsets_hbm, mixed, factor_out, whitened,
    panel, signs, sources, offsets, table, send, arrived, back, counts, parts, acc, acc2, first_sums, second_sums, picked, slots, relay, incoming,
    out_send, out_recv, back_send, back_recv, one_send, one_recv, two_send, two_recv,
    line_send, line_recv, plane_send, plane_recv, load_sem, ready,
):
    z, x, c, y = position()
    me = flat(z, x, c, y)
    barrier = pltpu.get_barrier_semaphore()
    loads = [
        pltpu.make_async_copy(panel_hbm.at[pl.ds(8 * g, 8)], panel.at[pl.ds(8 * g, 8)], load_sem.at[g]) for g in range(8)
    ]
    tables = [
        pltpu.make_async_copy(src, dst, load_sem.at[8 + i])
        for i, (src, dst) in enumerate(((signs_hbm, signs), (sources_hbm, sources), (offsets_hbm, offsets)))
    ]
    for load in tables[:1] + loads + tables[1:]:
        load.start()

    def signal_all(sem, peers, count):
        def step(t, carry):
            pl.semaphore_signal(sem, inc=1, device_id=device(*peers(t)), device_id_type=MESH)
            return carry

        lax.fori_loop(1, count, step, 0)

    signal_all(barrier, in_line, 8)
    signal_all(barrier, in_plane, 16)
    table[...] = lane_table()
    rows = lambda part: pl.ds(part * ROWS, ROWS)

    def send_out(part, groups):
        for group, low, high in groups:

            def step(t, carry):
                where = group(t)
                start(send.at[flat(*where), rows(part)], arrived.at[me, rows(part)], out_send.at[part], out_recv.at[part], where)
                return carry

            run(low, high, step)

    def send_back(part, groups):
        for group, low, high in groups:

            def step(t, carry):
                where = group(t)
                start(arrived.at[flat(*where), rows(part)], back.at[me, rows(part)], back_send.at[part], back_recv.at[part], where)
                return carry

            run(low, high, step)

    tables[0].wait()
    for part in range(PARTS):
        for g in range(8):
            if (g % 4) * 8 // ROWS == part:
                loads[g].wait()
        local_mix(part, panel, signs, table, send)
        if part == 0:
            pl.semaphore_wait(barrier, 22)
            signal_all(ready, in_plane, 16)
        send_out(part, GROUPS[:2])
    pl.semaphore_wait(ready, 15)
    for part in range(PARTS):
        send_out(part, GROUPS[2:])
        arrived[me, rows(part)] = send[me, rows(part)]
    tables[1].wait()
    tables[2].wait()
    count_rows(sources, offsets, counts, me)
    places = slot_places(sources, offsets, me)
    for part in range(PARTS):
        settle(arrived.at[pl.ds(0, 127), rows(part)], out_send.at[part], out_recv.at[part])
        combine(part, arrived)
        if part == 0:
            send_back(0, GROUPS[2:] + GROUPS[:2])
        else:
            send_back(1, ((elsewhere, 0, 49),))
        back[me, rows(part)] = arrived[me, rows(part)]
        if part == 0:
            gram_first(arrived, counts, parts, acc)
    gram_second(arrived, counts, parts, acc2)
    line, plane = c * 4 + y, z * 4 + x
    first_sums[line] = gram(acc, acc2)

    def send_sums(sums, at, peers, count, send_sem, recv_sem):
        def step(t, carry):
            start(sums.at[at], sums.at[at], send_sem, recv_sem, peers(t))
            return carry

        lax.fori_loop(1, count, step, 0)

    send_sums(first_sums, line, in_line, 8, one_send, one_recv)
    send_back(1, ((elsewhere, 49, 105),) + GROUPS[:2])
    for part in range(PARTS - 1):
        settle(back.at[pl.ds(0, 127), rows(part)], back_send.at[part], back_recv.at[part])
        unpack_part(part, back, mixed, 2.0**-10)
        pick_part(part, mixed, places, picked)
    settle(first_sums.at[pl.ds(0, 7)], one_send, one_recv)
    total = first_sums[0]
    for i in range(1, 8):
        total = total + first_sums[i]
    second_sums[plane] = total
    send_sums(second_sums, plane, in_plane, 16, two_send, two_recv)
    last = PARTS - 1
    settle(back.at[pl.ds(0, 127), rows(last)], back_send.at[last], back_recv.at[last])
    unpack_part(last, back, mixed, 2.0**-10)
    pick_part(last, mixed, places, picked)
    pack_slots([picked[r] for r in range(CAP)], slots)

    def step_line(t, carry):
        _, _, pc, py = where = in_line(t)
        start(slots.at[:, pc * 4 + py], relay.at[line], line_send, line_recv, where)
        return carry

    lax.fori_loop(1, 8, step_line, 0)
    relay[line] = slots[:, line]
    own = sources[pl.ds(me, 1), :]
    settle(second_sums.at[pl.ds(0, 15)], two_send, two_recv)
    total = second_sums[0]
    for i in range(1, 16):
        total = total + second_sums[i]
    state = eliminate(bordered(jnp.concatenate([total[:, :64], total[:, 64:]], axis=0) * (2.0**-34)), 0, MIDDLE)
    settle(relay.at[pl.ds(0, 7)], line_send, line_recv)

    def step_plane(t, carry):
        pz, px, _, _ = where = in_plane(t)
        start(relay.at[:, pz * 4 + px], incoming.at[plane], plane_send, plane_recv, where)
        return carry

    lax.fori_loop(1, 16, step_plane, 0)
    incoming[plane] = relay[:, plane]
    both = factors(eliminate(state, MIDDLE, COLS))
    factor_out[...] = both[:, :64]
    settle(incoming.at[pl.ds(0, 15)], plane_send, plane_recv)
    whitened[...] = exact6(both[:, 64:], place_samples(incoming, own), dot_nn)


def pass_on(mixed_in, factor_in, whitened_in, mixed, factor_out, whitened, sems):
    pairs = [(mixed_in.at[pl.ds(8 * g, 8)], mixed.at[pl.ds(8 * g, 8)]) for g in range(8)]
    pairs += [(factor_in, factor_out), (whitened_in, whitened)]
    copies = [pltpu.make_async_copy(src, dst, sems.at[i]) for i, (src, dst) in enumerate(pairs)]
    for copy in copies:
        copy.start()
    for copy in copies:
        copy.wait()


def local(panel, signs, sample_device, sample_offset):
    shape = lambda *dims: jax.ShapeDtypeStruct(dims, F32)
    vmem = pl.BlockSpec(memory_space=pltpu.VMEM)
    dma = pltpu.SemaphoreType.DMA
    made = pl.pallas_call(
        kernel,
        out_shape=(shape(64, 8192), shape(64, 64), shape(64, 128)),
        in_specs=[pl.BlockSpec(memory_space=pltpu.HBM)] * 4,
        out_specs=(vmem, vmem, vmem),
        scratch_shapes=[
            pltpu.VMEM((64, 8192), F32),
            pltpu.VMEM((1, 8192), I32),
            pltpu.VMEM((128, 128), I32),
            pltpu.VMEM((128, 128), I32),
            pltpu.VMEM((256, 256), BF16),
            pltpu.VMEM((DEVS, HALF, LANES), F32),
            pltpu.VMEM((DEVS, HALF, LANES), F32),
            pltpu.VMEM((DEVS, HALF, LANES), F32),
            pltpu.VMEM((64, 128), F32),
            pltpu.VMEM((32, 96, 256), BF16),
            pltpu.VMEM((96, 96), F32),
            pltpu.VMEM((192, 96), F32),
            pltpu.VMEM((8, 32, 128), F32),
            pltpu.VMEM((16, 32, 128), F32),
            pltpu.VMEM((CAP, 64, 128), F32),
            pltpu.VMEM((16, 8, 2, LANES), F32),
            pltpu.VMEM((8, 16, 2, LANES), F32),
            pltpu.VMEM((16, 8, 2, LANES), F32),
            dma((PARTS,)), dma((PARTS,)), dma((PARTS,)), dma((PARTS,)),
            dma, dma, dma, dma, dma, dma, dma, dma, dma((11,)), pltpu.SemaphoreType.REGULAR,
        ],
        compiler_params=pltpu.CompilerParams(collective_id=0, has_side_effects=True, vmem_limit_bytes=20 << 20),
    )(*(pltpu.with_memory_space_constraint(v, pltpu.HBM) for v in (panel, signs.reshape(1, -1), sample_device.reshape(128, 128), sample_offset.reshape(128, 128))))
    anywhere = pl.BlockSpec(memory_space=pl.ANY)
    return pl.pallas_call(
        pass_on,
        out_shape=(shape(64, 8192), shape(64, 64), shape(64, 128)),
        in_specs=[vmem, vmem, vmem],
        out_specs=(anywhere, anywhere, anywhere),
        scratch_shapes=[dma((10,))],
        compiler_params=pltpu.CompilerParams(vmem_limit_bytes=8 << 20),
    )(*made)


def solution(mesh):
    return jax.shard_map(
        local,
        mesh=mesh,
        in_specs=(P(None, AXES), P(AXES), P(), P()),
        out_specs=(P(None, AXES), P(), P(None, AXES)),
        check_vma=False,
    )
```

```python
import jax
import jax.numpy as jnp
from jax import lax
from jax.experimental import pallas as pl
from jax.experimental.pallas import tpu as pltpu
from jax.sharding import PartitionSpec as P

F32, BF16, I32 = jnp.float32, jnp.bfloat16, jnp.int32
AXES = ("rows", "sk")
DEVS, COLS, HALF, LANES, CAP = 128, 64, 32, 128, 4


def split3(x):
    top = x.astype(BF16)
    rest = x - top.astype(F32)
    mid = rest.astype(BF16)
    low = (rest - mid.astype(F32)).astype(BF16)
    return top, mid, low


def dot_nn(a, b):
    return lax.dot_general(a, b, (((1,), (0,)), ((), ())), preferred_element_type=F32)


def dot_nt(a, b):
    return lax.dot_general(a, b, (((1,), (1,)), ((), ())), preferred_element_type=F32)


def dot_tn(a, b):
    return lax.dot_general(a, b, (((0,), (0,)), ((), ())), preferred_element_type=F32)


def iota(shape, dim):
    return lax.broadcasted_iota(I32, shape, dim)


def butterflies(values):
    size, step = len(values), 1
    while step < size:
        nxt = list(values)
        for i in range(size):
            if not i & step:
                nxt[i] = values[i] + values[i + step]
                nxt[i + step] = values[i] - values[i + step]
        values, step = nxt, step * 2
    return values


def lane_table():
    k, n = iota((256, 256), 0), iota((256, 256), 1)
    bits = jnp.bitwise_and(k % 128, (n // 128) * 64 + n % 64)
    for shift in (4, 2, 1):
        bits = jnp.bitwise_xor(bits, lax.shift_right_logical(bits, shift))
    sign = 1.0 - 2.0 * jnp.bitwise_and(bits, 1).astype(F32)
    return jnp.where(k // 128 == (n % 128) // 64, sign, 0.0).astype(BF16)
MIDDLE = 16


PARTS = 2
LOWS, SIZES = (0, 16), (16, 16)
MESH = pl.DeviceIdType.MESH


def local_mix(part, panel, signs, table, send):
    base, size = LOWS[part], SIZES[part]
    at_rows = pl.ds(base, size)

    def first(high, carry):
        at = pl.ds(pl.multiple_of(high * 1024, 1024), 1024)
        sign = signs[:, at].astype(F32)
        upper = panel[base : base + size, at] * sign
        lower = panel[HALF + base : HALF + base + size, at] * sign
        lhs = jnp.concatenate(
            [
                jnp.concatenate([upper[:, 128 * b : 128 * b + 128], lower[:, 128 * b : 128 * b + 128]], axis=1)
                for b in range(8)
            ],
            axis=0,
        )
        weights = table[...]
        top, mid, low = split3(lhs)
        out = dot_nn(low, weights) + dot_nn(mid, weights) + dot_nn(top, weights)
        done = butterflies([out[size * b : size * b + size] for b in range(8)])
        for b in range(8):
            send[16 * high + 2 * b, at_rows] = done[b][:, :128]
            send[16 * high + 2 * b + 1, at_rows] = done[b][:, 128:]
        return carry

    lax.fori_loop(0, 8, first, 0)

    def second(low, carry):
        done = butterflies([send[16 * high + low, at_rows] for high in range(8)])
        for high in range(8):
            send[16 * high + low, at_rows] = done[high]
        return carry

    lax.fori_loop(0, 16, second, 0)


def combine(part, data):
    base, size = LOWS[part], SIZES[part]

    def first(i, carry):
        high, group = i // (size // 8), i % (size // 8)
        at = pl.ds(pl.multiple_of(base + group * 8, 8), 8)
        done = butterflies([data[16 * high + low, at] for low in range(16)])
        for low in range(16):
            data[16 * high + low, at] = done[low]
        return carry

    lax.fori_loop(0, size, first, 0)
    at_rows = pl.ds(base, size)

    def second(low, carry):
        done = butterflies([data[16 * high + low, at_rows] for high in range(8)])
        for high in range(8):
            data[16 * high + low, at_rows] = done[high]
        return carry

    lax.fori_loop(0, 16, second, 0)


def count_rows(sources, offsets, counts, me):
    counts[...] = jnp.zeros_like(counts)

    def step(i, carry):
        at = pl.ds(pl.multiple_of(i * 8, 8), 8)
        src8, rel8 = sources[at, :], offsets[at, :] - me * 64
        inside = jnp.logical_and(rel8 >= 0, rel8 < 64)
        lane8 = jnp.where(inside, rel8 + jnp.where(src8 >= 64, 64, 0), -1)
        q8 = jnp.bitwise_and(src8, 63)
        total = counts[...]
        for pair in range(4):
            q = jnp.concatenate([q8[2 * pair : 2 * pair + 1], q8[2 * pair + 1 : 2 * pair + 2]], axis=1)
            lane = jnp.concatenate([lane8[2 * pair : 2 * pair + 1], lane8[2 * pair + 1 : 2 * pair + 2]], axis=1)
            left = jnp.where(iota((64, 256), 0) == q, 1.0, 0.0).astype(BF16)
            right = jnp.where(iota((128, 256), 0) == lane, 1.0, 0.0).astype(BF16)
            total = total + dot_nt(left, right)
        counts[...] = total
        return carry

    lax.fori_loop(0, 16, step, 0)
    counts[...] = jnp.sqrt(counts[...])


def weighted_parts(part, data, roots, i):
    base, size = LOWS[part], SIZES[part]
    left = iota((size, LANES), 1) < 64
    pieces = []
    for q in (2 * i, 2 * i + 1):
        one, two = data[q, pl.ds(base, size)], data[q + 64, pl.ds(base, size)]
        upper = jnp.where(left, one, pltpu.roll(two, 64, 1))
        lower = jnp.where(left, pltpu.roll(one, 64, 1), two)
        pieces.append(jnp.concatenate([upper, lower], axis=0) * roots[pl.ds(q, 1), :])
    return jnp.concatenate(split3(jnp.concatenate(pieces, axis=1)), axis=0)


def gram_first(data, roots, parts, acc):
    acc[...] = jnp.zeros_like(acc)

    def step(i, carry):
        total = acc[...]
        for k in range(4):
            own = weighted_parts(0, data, roots, 4 * i + k)
            parts[4 * i + k] = own
            total = total + dot_nt(own, own)
        acc[...] = total
        return carry

    lax.fori_loop(0, 8, step, 0)


def gram_second(data, roots, parts, acc):
    acc[...] = jnp.zeros_like(acc)

    def step(i, carry):
        total = acc[...]
        for k in range(4):
            own = weighted_parts(1, data, roots, 4 * i + k)
            total = total + dot_nt(jnp.concatenate([parts[4 * i + k], own], axis=0), own)
        acc[...] = total
        return carry

    lax.fori_loop(0, 8, step, 0)


def merge_parts(acc, row, m, n):
    block = lambda i, j: acc[row + m * i : row + m * i + m, n * j : n * j + n]
    small = block(2, 2) + (block(1, 2) + block(2, 1))
    small = small + (block(0, 2) + block(2, 0)) + block(1, 1)
    return small + (block(0, 1) + block(1, 0)) + block(0, 0)


def gram(first, second):
    m, n = 2 * SIZES[0], 2 * SIZES[1]
    same, cross, last = merge_parts(first, 0, m, m), merge_parts(second, 0, m, n), merge_parts(second, 3 * m, n, n)
    g = jnp.concatenate(
        [jnp.concatenate([same, cross], axis=1), jnp.concatenate([cross.T, last], axis=1)], axis=0
    )
    spans = ((0, m // 2), (m, m + n // 2), (m // 2, m), (m + n // 2, m + n))
    swap = lambda v, dim: jnp.concatenate([lax.slice_in_dim(v, low, high, axis=dim) for low, high in spans], axis=dim)
    g = swap(swap(g, 0), 1)
    return jnp.concatenate([g[:32], g[32:]], axis=1)


def bordered(g):
    return jnp.concatenate([g, jnp.where(iota((COLS, 64), 0) == iota((COLS, 64), 1), 1.0, 0.0)], axis=1)


def eliminate(m, low, high):
    subs = iota((COLS, 1), 0)
    for j in range(low, high):
        pivot_row = m[j : j + 1, :]
        inverse = 1.0 / m[j : j + 1, j : j + 1]
        lead = jnp.where(subs > j, m[:, j : j + 1] * inverse, 0.0)
        m = m - lead * pivot_row
    return m


def factors(m):
    sub, lane = iota((COLS, LANES), 0), iota((COLS, LANES), 1)
    diagonal = jnp.sum(jnp.where(sub == lane, m, 0.0), axis=1, keepdims=True)
    scaled = m / jnp.sqrt(diagonal)
    return jnp.where(jnp.logical_or(lane >= sub, lane >= 64), scaled, 0.0)


def earlier():
    return jnp.where(iota((128, 128), 0) < iota((128, 128), 1), 1.0, 0.0).astype(BF16)


def slot_places(sources, offsets, me):
    mine = sources[...] == me
    rank = dot_nn(jnp.where(mine, 1.0, 0.0).astype(BF16), earlier())
    high = (offsets[...] // 128).astype(F32)
    low = (offsets[...] % 128).astype(F32)
    ones = jnp.ones((8, 128), BF16)
    places = []
    for r in range(CAP):
        chosen = jnp.logical_and(mine, rank == float(r))
        places.append(
            tuple(dot_nt(ones, jnp.where(chosen, v, 0.0).astype(BF16)).astype(I32) for v in (high, low))
        )
    return places


def unpack_part(part, back, mixed, scale):
    base, size = LOWS[part], SIZES[part]
    left = iota((size, LANES), 1) < 64

    def step(i, carry):
        for k in range(16):
            b = 16 * i + k
            at = pl.ds(pl.multiple_of(b * 128, 128), 128)
            one, two = back[2 * b, pl.ds(base, size)], back[2 * b + 1, pl.ds(base, size)]
            upper = jnp.where(left, one, pltpu.roll(two, 64, 1))
            lower = jnp.where(left, pltpu.roll(one, 64, 1), two)
            mixed[base : base + size, at] = upper * scale
            mixed[HALF + base : HALF + base + size, at] = lower * scale
        return carry

    lax.fori_loop(0, 4, step, 0)


def pick_part(part, mixed, places, picked):
    bases = [half + LOWS[part] + 8 * k for half in (0, HALF) for k in range(SIZES[part] // 8)]
    for r, (high, low) in enumerate(places):

        def step(i, found):
            for k in range(64):
                b = 64 * i + k
                at = pl.ds(pl.multiple_of(b * 128, 128), 128)
                here = high == b
                found = tuple(
                    jnp.where(
                        here,
                        jnp.take_along_axis(mixed[base : base + 8, at], low, axis=1, mode="promise_in_bounds"),
                        old,
                    )
                    for base, old in zip(bases, found)
                )
            return found

        done = lax.fori_loop(0, 1, step, tuple(jnp.zeros((8, LANES), F32) for _ in bases))
        for base, value in zip(bases, done):
            picked[r, base : base + 8] = value


def exact6(a, b, dot):
    a1, a2, a3 = split3(a)
    b1, b2, b3 = split3(b)
    small = dot(a2, b2) + (dot(a1, b3) + dot(a3, b1))
    return small + (dot(a1, b2) + dot(a2, b1)) + dot(a1, b1)


def pack_slots(picked, out):
    for pair in range(2):
        both = jnp.concatenate([picked[2 * pair].T, picked[2 * pair + 1].T], axis=1)
        out[:, :, pair, :] = both.reshape(16, 8, LANES)


def place_samples(incoming, own):
    hot = iota((128, 128), 0) == own
    flag = jnp.where(hot, 1.0, 0.0)
    rank = dot_nn(flag.astype(BF16), earlier())
    total = jnp.zeros((COLS, LANES), F32)
    for pair in range(2):
        top, mid, low = split3(incoming[:, :, pair, :].reshape(DEVS, LANES))
        for half in range(2):
            chosen = jnp.where(rank == float(2 * pair + half), flag, 0.0).astype(BF16)
            got = dot_tn(low, chosen) + dot_tn(mid, chosen) + dot_tn(top, chosen)
            total = total + got[64 * half : 64 * half + 64]
    return total


def position():
    row, y = lax.axis_index("rows"), lax.axis_index("sk")
    return row // 8, (row // 2) % 4, row % 2, y


def device(z, x, c, y):
    return ((z * 4 + x) * 2 + c, y)


def flat(z, x, c, y):
    return ((z * 4 + x) * 2 + c) * 4 + y


def in_line(t):
    z, x, c, y = position()
    return z, x, (c + t) % 2, (y + t // 2) % 4


def in_plane(t):
    z, x, c, y = position()
    return (z + t // 4 + t) % 4, (x + t) % 4, c, y


def elsewhere(i):
    z, x, _, _ = in_plane(1 + i % 15)
    _, _, c, y = in_line(1 + i % 7)
    return z, x, c, y


def run(low, high, step):
    whole = (high - low) // 7

    def several(i, carry):
        for k in range(7):
            step(low + 7 * i + k, 0)
        return carry

    lax.fori_loop(0, whole, several, 0)
    for t in range(low + 7 * whole, high):
        step(t, 0)


GROUPS = ((in_line, 1, 8), (in_plane, 1, 16), (elsewhere, 0, 105))


def start(src, dst, send_sem, recv_sem, where):
    pltpu.make_async_remote_copy(
        src_ref=src, dst_ref=dst, send_sem=send_sem, recv_sem=recv_sem, device_id=device(*where), device_id_type=MESH
    ).start()


def settle(ref, send_sem, recv_sem):
    whole = pltpu.make_async_remote_copy(
        src_ref=ref, dst_ref=ref, send_sem=send_sem, recv_sem=recv_sem, device_id=device(*in_line(1)), device_id_type=MESH
    )
    whole.wait_recv()
    whole.wait_send()


def kernel(
    panel_hbm, signs_hbm, sources_hbm, offsets_hbm, mixed, factor_out, whitened,
    panel, signs, sources, offsets, table, send, arrived, back, counts, parts, acc, acc2, first_sums, second_sums, picked, slots, relay, incoming,
    out_send, out_recv, back_send, back_recv, one_send, one_recv, two_send, two_recv,
    line_send, line_recv, plane_send, plane_recv, load_sem, ready,
):
    z, x, c, y = position()
    me = flat(z, x, c, y)
    barrier = pltpu.get_barrier_semaphore()
    loads = [
        pltpu.make_async_copy(panel_hbm.at[pl.ds(8 * g, 8)], panel.at[pl.ds(8 * g, 8)], load_sem.at[g]) for g in range(8)
    ]
    tables = [
        pltpu.make_async_copy(src, dst, load_sem.at[8 + i])
        for i, (src, dst) in enumerate(((signs_hbm, signs), (sources_hbm, sources), (offsets_hbm, offsets)))
    ]
    for load in tables[:1] + loads + tables[1:]:
        load.start()

    def signal_all(sem, peers, count):
        def step(t, carry):
            pl.semaphore_signal(sem, inc=1, device_id=device(*peers(t)), device_id_type=MESH)
            return carry

        lax.fori_loop(1, count, step, 0)

    signal_all(barrier, in_line, 8)
    signal_all(barrier, in_plane, 16)
    table[...] = lane_table()
    rows = lambda part: pl.ds(LOWS[part], SIZES[part])

    def send_out(part, groups):
        for group, low, high in groups:

            def step(t, carry):
                where = group(t)
                start(send.at[flat(*where), rows(part)], arrived.at[me, rows(part)], out_send.at[part], out_recv.at[part], where)
                return carry

            run(low, high, step)

    def send_back(part, groups):
        for group, low, high in groups:

            def step(t, carry):
                where = group(t)
                start(arrived.at[flat(*where), rows(part)], back.at[me, rows(part)], back_send.at[part], back_recv.at[part], where)
                return carry

            run(low, high, step)

    tables[0].wait()
    for part in range(PARTS):
        for g in range(8):
            if 0 <= (g % 4) * 8 - LOWS[part] < SIZES[part]:
                loads[g].wait()
        local_mix(part, panel, signs, table, send)
        if part == 0:
            pl.semaphore_wait(barrier, 22)
            signal_all(ready, in_plane, 16)
        send_out(part, GROUPS[:2])
    pl.semaphore_wait(ready, 15)
    for part in range(PARTS):
        send_out(part, GROUPS[2:])
        arrived[me, rows(part)] = send[me, rows(part)]
    tables[1].wait()
    tables[2].wait()
    count_rows(sources, offsets, counts, me)
    places = slot_places(sources, offsets, me)
    for part in range(PARTS):
        settle(arrived.at[pl.ds(0, 127), rows(part)], out_send.at[part], out_recv.at[part])
        combine(part, arrived)
        if part == 0:
            send_back(0, GROUPS[2:] + GROUPS[:2])
        else:
            send_back(1, ((elsewhere, 0, 49),))
        back[me, rows(part)] = arrived[me, rows(part)]
        if part == 0:
            gram_first(arrived, counts, parts, acc)
    gram_second(arrived, counts, parts, acc2)
    line, plane = c * 4 + y, z * 4 + x
    first_sums[line] = gram(acc, acc2)

    def send_sums(sums, at, peers, count, send_sem, recv_sem):
        def step(t, carry):
            start(sums.at[at], sums.at[at], send_sem, recv_sem, peers(t))
            return carry

        lax.fori_loop(1, count, step, 0)

    send_sums(first_sums, line, in_line, 8, one_send, one_recv)
    send_back(1, ((elsewhere, 49, 105),) + GROUPS[:2])
    for part in range(PARTS - 1):
        settle(back.at[pl.ds(0, 127), rows(part)], back_send.at[part], back_recv.at[part])
        unpack_part(part, back, mixed, 2.0**-10)
        pick_part(part, mixed, places, picked)
    settle(first_sums.at[pl.ds(0, 7)], one_send, one_recv)
    total = first_sums[0]
    for i in range(1, 8):
        total = total + first_sums[i]
    second_sums[plane] = total
    send_sums(second_sums, plane, in_plane, 16, two_send, two_recv)
    last = PARTS - 1
    settle(back.at[pl.ds(0, 127), rows(last)], back_send.at[last], back_recv.at[last])
    unpack_part(last, back, mixed, 2.0**-10)
    pick_part(last, mixed, places, picked)
    pack_slots([picked[r] for r in range(CAP)], slots)

    def step_line(t, carry):
        _, _, pc, py = where = in_line(t)
        start(slots.at[:, pc * 4 + py], relay.at[line], line_send, line_recv, where)
        return carry

    lax.fori_loop(1, 8, step_line, 0)
    relay[line] = slots[:, line]
    own = sources[pl.ds(me, 1), :]
    settle(second_sums.at[pl.ds(0, 15)], two_send, two_recv)
    total = second_sums[0]
    for i in range(1, 16):
        total = total + second_sums[i]
    state = eliminate(bordered(jnp.concatenate([total[:, :64], total[:, 64:]], axis=0) * (2.0**-34)), 0, MIDDLE)
    settle(relay.at[pl.ds(0, 7)], line_send, line_recv)

    def step_plane(t, carry):
        pz, px, _, _ = where = in_plane(t)
        start(relay.at[:, pz * 4 + px], incoming.at[plane], plane_send, plane_recv, where)
        return carry

    lax.fori_loop(1, 16, step_plane, 0)
    incoming[plane] = relay[:, plane]
    both = factors(eliminate(state, MIDDLE, COLS))
    factor_out[...] = both[:, :64]
    settle(incoming.at[pl.ds(0, 15)], plane_send, plane_recv)
    whitened[...] = exact6(both[:, 64:], place_samples(incoming, own), dot_nn)


def pass_on(mixed_in, factor_in, whitened_in, mixed, factor_out, whitened, sems):
    pairs = [(mixed_in.at[pl.ds(8 * g, 8)], mixed.at[pl.ds(8 * g, 8)]) for g in range(8)]
    pairs += [(factor_in, factor_out), (whitened_in, whitened)]
    copies = [pltpu.make_async_copy(src, dst, sems.at[i]) for i, (src, dst) in enumerate(pairs)]
    for copy in copies:
        copy.start()
    for copy in copies:
        copy.wait()


def local(panel, signs, sample_device, sample_offset):
    shape = lambda *dims: jax.ShapeDtypeStruct(dims, F32)
    vmem = pl.BlockSpec(memory_space=pltpu.VMEM)
    dma = pltpu.SemaphoreType.DMA
    made = pl.pallas_call(
        kernel,
        out_shape=(shape(64, 8192), shape(64, 64), shape(64, 128)),
        in_specs=[pl.BlockSpec(memory_space=pltpu.HBM)] * 4,
        out_specs=(vmem, vmem, vmem),
        scratch_shapes=[
            pltpu.VMEM((64, 8192), F32),
            pltpu.VMEM((1, 8192), I32),
            pltpu.VMEM((128, 128), I32),
            pltpu.VMEM((128, 128), I32),
            pltpu.VMEM((256, 256), BF16),
            pltpu.VMEM((DEVS, HALF, LANES), F32),
            pltpu.VMEM((DEVS, HALF, LANES), F32),
            pltpu.VMEM((DEVS, HALF, LANES), F32),
            pltpu.VMEM((64, 128), F32),
            pltpu.VMEM((32, 6 * SIZES[0], 256), BF16),
            pltpu.VMEM((6 * SIZES[0], 6 * SIZES[0]), F32),
            pltpu.VMEM((192, 6 * SIZES[1]), F32),
            pltpu.VMEM((8, 32, 128), F32),
            pltpu.VMEM((16, 32, 128), F32),
            pltpu.VMEM((CAP, 64, 128), F32),
            pltpu.VMEM((16, 8, 2, LANES), F32),
            pltpu.VMEM((8, 16, 2, LANES), F32),
            pltpu.VMEM((16, 8, 2, LANES), F32),
            dma((PARTS,)), dma((PARTS,)), dma((PARTS,)), dma((PARTS,)),
            dma, dma, dma, dma, dma, dma, dma, dma, dma((11,)), pltpu.SemaphoreType.REGULAR,
        ],
        compiler_params=pltpu.CompilerParams(collective_id=0, has_side_effects=True, vmem_limit_bytes=20 << 20),
    )(*(pltpu.with_memory_space_constraint(v, pltpu.HBM) for v in (panel, signs.reshape(1, -1), sample_device.reshape(128, 128), sample_offset.reshape(128, 128))))
    anywhere = pl.BlockSpec(memory_space=pl.ANY)
    return pl.pallas_call(
        pass_on,
        out_shape=(shape(64, 8192), shape(64, 64), shape(64, 128)),
        in_specs=[vmem, vmem, vmem],
        out_specs=(anywhere, anywhere, anywhere),
        scratch_shapes=[dma((10,))],
        compiler_params=pltpu.CompilerParams(vmem_limit_bytes=8 << 20),
    )(*made)


def solution(mesh):
    return jax.shard_map(
        local,
        mesh=mesh,
        in_specs=(P(None, AXES), P(AXES), P(), P()),
        out_specs=(P(None, AXES), P(), P(None, AXES)),
        check_vma=False,
    )
```
